512 devices in a mesh: ctx: 16 (over y, x_lo), exp: 32 (over x_hi, z, core).
Axes of the slice: x: 4 (x_hi: 2, x_lo: 2; x = x_hi * 2 + x_lo), y: 8, z: 8, core: 2. Of those that a mesh axis runs over, the one named last changes fastest.
Arguments:
- queries: bfloat16 [32, 1024, 2048], P('exp', 'ctx'), may hold values from -21 to 21
- keys: bfloat16 [32, 1024, 256], P('exp', 'ctx'), may hold values from -6 to 6
- values: bfloat16 [32, 1024, 256], P('exp', 'ctx'), may hold values from -4 to 4
- sinks: float32 [32], replicated, may hold values from -1 to 3
- out_weight: bfloat16 [2048, 1440], P('exp'), may hold values from -0.125 to 0.125
- norm_gain: float32 [1440], replicated, may hold values from 0.1 to 1.9
- routes: int32 [32, 1024, 4], P('exp', 'ctx'), may hold values from 0 to 15, all different within a row; in each aligned block of 64 rows (0 to 63, 64 to 127, ..., all dimensions but the last counted through in order) at most 20 rows name the same one
- gates: float32 [32, 1024, 4], P('exp', 'ctx'), may hold values from 0.1 to 1
- gate_codes: int32 [32, 1440, 192], P('exp'), may hold values from 0 to 65535, as said below
- up_codes: int32 [32, 1440, 192], P('exp'), may hold values from 0 to 65535, as said below
- down_codes: int32 [32, 768, 360], P('exp'), may hold values from 0 to 65535, as said below
- gate_scales: int32 [32, 45, 768], P('exp'), may hold values from 118 to 121
- up_scales: int32 [32, 45, 768], P('exp'), may hold values from 118 to 121
- down_scales: int32 [32, 24, 1440], P('exp'), may hold values from 118 to 121
Outputs:
- layer_out: bfloat16 [32, 1024, 1440], P('exp', 'ctx')
The draws below stay inside these ranges and needn't reach their ends.
Inputs may be any that keep to these rules, and one draw needn't show every extreme that they name: `routes`: each token names 4 different experts; within the tokens of one device (aligned blocks of 64 rows) no expert is named by more than 20 tokens, a bound that some block reaches. `gate_codes`: each word packs four 4-bit codes; code k lies in bits 4k to 4k+3 and belongs to hidden unit 4q+k of word column q. `up_codes`: each word packs four 4-bit codes; code k lies in bits 4k to 4k+3 and belongs to hidden unit 4q+k of word column q. `down_codes`: each word packs four 4-bit codes; code k lies in bits 4k to 4k+3 and belongs to feature 4q+k of word column q.
All inputs are finite; a program needn't handle non-finite values.
Results may differ from the reference program's by a relative error of at most 0.023.
Values may be sent and summed in bfloat16 or wider, within the bound.
A program may use at most 128 MiB of HBM per device.

```python
import math
import jax
import jax.numpy as jnp
import numpy as np
from jax import lax

D = 1440
QH = 32
KVH = 4
HD = 64
TOPK = 4
SPLIT = 2
TOK_DEV = 64
SEQ = 1024
SEQS = 32
EXPERTS = 16
SLICES = 32
FF_DEV = 768
CAP = 20
N_CTX = 16


def base_fields(key):
    key_field = jnp.clip(jax.random.normal(jax.random.fold_in(key, 7), (SEQS, SEQ, KVH * HD), jnp.float32), -4.0, 4.0)
    query_field = jnp.clip(jax.random.normal(jax.random.fold_in(key, 9), (SEQS, SEQ, QH * HD), jnp.float32), -4.0, 4.0)
    return (key_field, query_field)


def draw_keys(key, part):
    key_field, query_field = base_fields(key)
    return key_field.astype(jnp.bfloat16)


def draw_queries(key, part):
    key_field, query_field = base_fields(key)
    return query_field.astype(jnp.bfloat16)


def pack_codes(key, shape):
    codes_raw = jax.random.randint(key, shape + (4,), 0, 16, dtype=jnp.int32)
    packed = codes_raw[..., 0] + 16 * codes_raw[..., 1] + 256 * codes_raw[..., 2] + 4096 * codes_raw[..., 3]
    total = shape[0] * shape[1] * shape[2]
    flat = packed.reshape(total)
    high_spot = jax.random.randint(jax.random.fold_in(key, 31), (), 0, total // 2, dtype=jnp.int32)
    low_spot = jax.random.randint(jax.random.fold_in(key, 32), (), total // 2, total, dtype=jnp.int32)
    flat = flat.at[high_spot].set(65535)
    flat = flat.at[low_spot].set(0)
    return flat.reshape(shape)


def draw_gate_codes(key, part):
    return pack_codes(jax.random.fold_in(key, 21), (SLICES, D, FF_DEV // 4))


def draw_up_codes(key, part):
    return pack_codes(jax.random.fold_in(key, 22), (SLICES, D, FF_DEV // 4))


def draw_down_codes(key, part):
    return pack_codes(jax.random.fold_in(key, 23), (SLICES, FF_DEV, D // 4))


def with_ends(entries, key, least, largest):
    spot = [jax.random.randint(jax.random.fold_in(key, axis), (), 0, length) for axis, length in enumerate(entries.shape)]
    longest = entries.shape.index(max(entries.shape))
    neighbour = spot[:longest] + [(spot[longest] + 1) % entries.shape[longest]] + spot[longest + 1:]
    return entries.at[tuple(spot)].set(least).at[tuple(neighbour)].set(largest)


def block_scale(rng, dims, shards, low, largest):
    def one(dim, parts):
        steps = jax.random.uniform(jax.random.fold_in(jax.random.fold_in(rng, 6), dim), (parts,), jnp.float32, low / len(shards), largest / len(shards))
        return jnp.repeat(jnp.exp(steps), dims[dim] // parts).reshape((-1,) + (1,) * (len(dims) - dim - 1))

    factor_of = one(*shards[0])
    for cut in shards[1:]:
        factor_of = factor_of * one(*cut)
    return factor_of


def routed_block(stream_key, own, number, rows, amount, top, limit, skew):
    sequence = jax.random.permutation(stream_key, amount)
    crowded, usual = portions_of(amount, rows * top, limit, skew, True), portions_of(amount, rows * top, limit, skew, False)
    places = jnp.arange(amount)

    def named(lengths, rotation):
        used = int((lengths > 0).sum())
        fixed = max(1, used // 4)
        passed = fixed + (places - fixed + rotation * (used - fixed)) % max(1, amount - fixed)
        return jnp.zeros((amount,), jnp.int32).at[sequence[jnp.where(places < fixed, places, passed)]].set(jnp.asarray(lengths, jnp.int32))

    lengths = jnp.where(number % 4 == 0, named(crowded, number // 4), named(usual, number - number // 4 - 1))
    mixed = jax.random.permutation(jax.random.fold_in(own, 3), amount)
    source_of, taker = mixed[0:amount // 2 * 2:2], mixed[1:amount // 2 * 2:2]
    slack = jnp.minimum(lengths[source_of] - 1, limit - lengths[taker]) // 2
    slack = jnp.where((source_of == sequence[0]) | (taker == sequence[0]) | (lengths[taker] == 0), 0, jnp.maximum(slack, 0))
    passed = jax.random.randint(jax.random.fold_in(own, 4), (amount // 2,), 0, 1 << 20) % (slack + 1)
    lengths = lengths.at[source_of].add(-passed).at[taker].add(passed)
    labels = jnp.searchsorted(jnp.cumsum(lengths), jnp.arange(rows * top), side="right").astype(jnp.int32)
    table = labels.reshape(top, rows).T
    table = table[jax.random.permutation(jax.random.fold_in(own, 1), rows)]
    rotation = jax.random.randint(jax.random.fold_in(own, 2), (rows, 1), 0, top)
    return jnp.take_along_axis(table, (jnp.arange(top)[None, :] + rotation) % top, axis=1)


def portions_of(count, total, limit, skew, full):
    loads = [(1 << 20) // math.isqrt(grade ** skew) + 1 for grade in range(1, count + 1)]
    largest = limit if full else min(limit, max(-(-total // count), total * loads[0] // sum(loads)))
    least = 1 if total - largest >= count - 1 else 0
    counts, rest = [largest] + [least] * (count - 1), total - largest - least * (count - 1)
    while rest > 0:
        movable = [i for i in range(1, count) if counts[i] < largest] or [i for i in range(1, count) if counts[i] < limit]
        mass, left = sum([loads[i] for i in movable]), rest
        for i in movable:
            extra = min(limit - counts[i], max(1, left * loads[i] // mass), rest)
            counts[i] = counts[i] + extra
            rest = rest - extra
    return np.array(counts)


def centred(stream_key, shape, width, most, pieces=(), kind=jnp.bfloat16):
    loudness = block_scale(stream_key, shape, pieces, -0.22, 0.18) if pieces else 1.0
    values = jax.random.normal(stream_key, shape, jnp.float32) * width * loudness
    return jnp.minimum(jnp.maximum(values, -most), most).astype(kind)


def setup_inputs(seed: int = 0) -> dict:
    streams_of = jax.random.split(jax.random.key(seed), 15)
    queries = draw_queries(jax.random.fold_in(streams_of[14], 71), 0)
    keys = draw_keys(jax.random.fold_in(streams_of[14], 71), 0)
    values = centred(streams_of[2], (SEQS, SEQ, KVH * HD), 1.0, 4.0, ((0, 32), (1, 16)))
    sinks = jnp.clip(jax.random.uniform(streams_of[3], (QH,), jnp.float32, -1.0, 3.0), -1.0, 3.0)
    out_weight = centred(streams_of[4], (QH * HD, D), (QH * HD) ** -0.5, 0.125, ((0, 32),))
    norm_gain = jnp.clip(1.0 + 0.18 * jax.random.normal(streams_of[5], (D,), jnp.float32), 0.1, 1.9)
    routes_keys = jax.random.split(jax.random.fold_in(streams_of[6], 1), SEQS * SEQ // TOK_DEV)
    routes_turns = jax.random.permutation(jax.random.fold_in(streams_of[6], 3), SEQS * SEQ // TOK_DEV)
    routes = jax.vmap(lambda own, number: routed_block(jax.random.fold_in(streams_of[6], 2), own, number, TOK_DEV, EXPERTS, TOPK, CAP, 1))(routes_keys, routes_turns).reshape((SEQS, SEQ, TOPK))
    gates = jnp.clip(jnp.exp(math.log(1.0) - 2.3025851 * jax.random.uniform(streams_of[7], (SEQS, SEQ, TOPK), jnp.float32) ** block_scale(streams_of[7], (SEQS, SEQ, TOPK), ((0, 32), (1, 16)), -0.2, 0.2)), 0.1, 1.0)
    gate_codes = draw_gate_codes(jax.random.fold_in(streams_of[14], 71), 0)
    up_codes = draw_up_codes(jax.random.fold_in(streams_of[14], 71), 0)
    down_codes = draw_down_codes(jax.random.fold_in(streams_of[14], 71), 0)
    gate_scales = with_ends(jax.random.randint(streams_of[11], (SLICES, D // 32, FF_DEV), 118, 122), jax.random.fold_in(streams_of[11], 1), 118, 121).astype(jnp.int32)
    up_scales = with_ends(jax.random.randint(streams_of[12], (SLICES, D // 32, FF_DEV), 118, 122), jax.random.fold_in(streams_of[12], 1), 118, 121).astype(jnp.int32)
    down_scales = with_ends(jax.random.randint(streams_of[13], (SLICES, FF_DEV // 32, D), 118, 122), jax.random.fold_in(streams_of[13], 1), 118, 121).astype(jnp.int32)
    return dict(queries=queries, keys=keys, values=values, sinks=sinks, out_weight=out_weight, norm_gain=norm_gain, routes=routes, gates=gates, gate_codes=gate_codes, up_codes=up_codes, down_codes=down_codes, gate_scales=gate_scales, up_scales=up_scales, down_scales=down_scales)


def decode_block(codes, scales):
    shifts = jnp.array([0, 4, 8, 12], dtype=jnp.int32)
    nibble = jnp.right_shift(codes[..., None], shifts) & 15
    nibble = nibble.reshape(codes.shape[0], codes.shape[1] * 4)
    magnitude = nibble & 7
    mag_float = magnitude.astype(jnp.float32)
    levels = jnp.where(magnitude < 2, 0.5 * mag_float, jnp.exp2(jnp.right_shift(magnitude, 1).astype(jnp.float32) - 1.0) * (1.0 + 0.5 * (magnitude & 1).astype(jnp.float32)))
    signed = jnp.where(nibble >= 8, -levels, levels)
    factor = jnp.exp2(jnp.repeat(scales, 32, axis=0).astype(jnp.float32) - 127.0)
    return (signed * factor).astype(jnp.bfloat16)

def expert_rows(slot_rows, w_gate, w_up, w_down):
    flat_rows = slot_rows.reshape(-1, slot_rows.shape[-1])
    gate_act = jnp.dot(flat_rows, w_gate, preferred_element_type=jnp.float32)
    up_act = jnp.dot(flat_rows, w_up, preferred_element_type=jnp.float32)
    active = ((up_act + 1.0) * gate_act * jax.nn.sigmoid(1.702 * gate_act)).astype(jnp.bfloat16)
    result = jnp.dot(active, w_down, preferred_element_type=jnp.float32).astype(jnp.bfloat16)
    return result.reshape(slot_rows.shape)

def reference(queries, keys, values, sinks, out_weight, norm_gain, routes, gates, gate_codes, up_codes, down_codes, gate_scales, up_scales, down_scales):
    groups = QH // KVH
    scale = 1.0 / math.sqrt(HD)
    head_sinks = sinks.reshape(KVH, groups)

    def one_sequence(items):
        query_seq, key_seq, value_seq = items
        grouped = query_seq.reshape(SEQ, KVH, groups, HD).astype(jnp.float32)
        key_heads = key_seq.reshape(SEQ, KVH, HD).astype(jnp.float32)
        value_heads = value_seq.reshape(SEQ, KVH, HD).astype(jnp.float32)
        scores = jnp.einsum('qhsd,khd->hsqk', grouped, key_heads) * scale
        causal = jnp.arange(SEQ)[:, None] >= jnp.arange(SEQ)[None, :]
        scores = jnp.where(causal[None, None], scores, -1e+30)
        row_top = jnp.maximum(lax.optimization_barrier(jnp.max(scores, axis=-1)), head_sinks[:, :, None])
        weights = jnp.exp(scores - row_top[..., None])
        denominator = jnp.exp(head_sinks[:, :, None] - row_top) + lax.optimization_barrier(jnp.sum(weights, axis=-1))
        rounded = lax.optimization_barrier(weights.astype(jnp.bfloat16)).astype(jnp.float32)
        numerator = jnp.einsum('hsqk,khd->hsqd', rounded, value_heads)
        result = numerator / denominator[..., None]
        return jnp.transpose(result, (2, 0, 1, 3)).reshape(SEQ, QH * HD).astype(jnp.bfloat16)
    attended = lax.map(one_sequence, (queries, keys, values))
    token_count = SEQS * SEQ
    branch = jnp.dot(attended.reshape(token_count, QH * HD), out_weight, preferred_element_type=jnp.float32)
    mean_sq = lax.optimization_barrier(jnp.mean(branch * branch, axis=-1, keepdims=True))
    normed = (branch * lax.rsqrt(mean_sq + 1e-05) * norm_gain).astype(jnp.bfloat16)
    route_ids = routes.reshape(-1)
    gate_flat = gates.reshape(-1)
    route_count = token_count * TOPK
    rows_cap = SEQS * N_CTX * CAP

    def one_expert(running, expert):
        hit_mask = route_ids == expert
        slot_order = jnp.cumsum(hit_mask.astype(jnp.int32)) - 1
        target = jnp.where(hit_mask, slot_order, rows_cap)
        slots = jnp.full((rows_cap,), route_count, jnp.int32).at[target].set(jnp.arange(route_count, dtype=jnp.int32), mode='drop')
        valid = slots < route_count
        safe_slot = jnp.minimum(slots, route_count - 1)
        token = safe_slot // TOPK
        slot_rows = normed[token]
        summed = jnp.zeros((rows_cap, D), jnp.float32)
        for part_index in range(SPLIT):
            slice_index = expert * SPLIT + part_index
            w_gate = decode_block(lax.dynamic_index_in_dim(gate_codes, slice_index, 0, False), lax.dynamic_index_in_dim(gate_scales, slice_index, 0, False))
            w_up = decode_block(lax.dynamic_index_in_dim(up_codes, slice_index, 0, False), lax.dynamic_index_in_dim(up_scales, slice_index, 0, False))
            w_down = decode_block(lax.dynamic_index_in_dim(down_codes, slice_index, 0, False), lax.dynamic_index_in_dim(down_scales, slice_index, 0, False))
            partial_value = expert_rows(slot_rows, w_gate, w_up, w_down)
            summed = summed + lax.optimization_barrier(partial_value).astype(jnp.float32)
        expert_out = lax.optimization_barrier(summed.astype(jnp.bfloat16)).astype(jnp.float32)
        gate_w = jnp.where(valid, gate_flat[safe_slot], 0.0)
        return (running.at[token].add(gate_w[:, None] * expert_out), None)
    mixed, _ = lax.scan(one_expert, jnp.zeros((token_count, D), jnp.float32), jnp.arange(EXPERTS, dtype=jnp.int32))
    return (branch + mixed).astype(jnp.bfloat16).reshape(SEQS, SEQ, D)
```

```python
import functools
import math

import jax
import jax.numpy as jnp
from jax import lax
from jax.experimental import pallas as pl
from jax.experimental.pallas import tpu as pltpu
from jax.sharding import PartitionSpec as P

QH = 32
KVH = 4
HD = 64
TOPK = 4
D = 1440
DP = 1536
FF = 768
TOK = 64
CHIPS = 16
BLK = 240
MESH = pl.DeviceIdType.MESH
F32 = jnp.float32
BF16 = jnp.bfloat16

OFFSETS = []
for step in range(8):
    half = (step + 1) // 2
    dz = half if step % 2 else -half
    OFFSETS += [(0, dz), (1, dz)]


def iota(shape, axis):
    return lax.broadcasted_iota(jnp.int32, shape, axis)


def dot(a, b):
    return jnp.dot(a, b, preferred_element_type=F32)


def offset_expert(i, x_hi, z):
    step = i >> 1
    half = (step + 1) >> 1
    dz = jnp.where((step & 1) == 1, half, -half)
    return ((x_hi + (i & 1)) & 1) * 8 + ((z + dz + 8) & 7)


def split3(x):
    hi = x.astype(BF16)
    rest = x - hi.astype(F32)
    mid = rest.astype(BF16)
    low = (rest - mid.astype(F32)).astype(BF16)
    return hi, mid, low


def fp4_plane(words, shift):
    code = (words >> shift) & 15
    size = code & 7
    twice = size + jnp.maximum(size - 4, 0) + 2 * jnp.maximum(size - 6, 0)
    return jnp.where(code >= 8, -twice, twice).astype(F32).astype(BF16)


def decode(codes_ref, scales_ref, planes_ref, perm_ref, out_ref, rows, words, m_rows):
    blocks = [(b, min(128, words - b)) for b in range(0, words, 128)]

    def planes_step(i, _):
        r = pl.multiple_of(i * 32, 32)
        for b, (lo, count) in enumerate(blocks):
            w = codes_ref[pl.ds(r, 32), lo : lo + count]
            if count == 128:
                for k in range(4):
                    planes_ref[pl.ds(r, 32), 512 * b + 128 * k : 512 * b + 128 * (k + 1)] = fp4_plane(w, 4 * k)
            elif count == 64:
                ww = jnp.concatenate([w, w], axis=1)
                high = (iota((32, 128), 1) >> 6) * 4
                for k in range(2):
                    planes_ref[pl.ds(r, 32), 512 * b + 128 * k : 512 * b + 128 * (k + 1)] = fp4_plane(ww, high + 8 * k)
            else:
                ww = jnp.concatenate([w, jnp.zeros((32, 128 - count), jnp.int32)], axis=1)
                for k in range(4):
                    planes_ref[pl.ds(r, 32), 512 * b + 128 * k : 512 * b + 128 * (k + 1)] = fp4_plane(ww, 4 * k)
        return 0

    lax.fori_loop(0, rows // 32, planes_step, 0)

    def product_step(i, _):
        r = pl.multiple_of(i * m_rows, 32)
        for b, (lo, count) in enumerate(blocks):
            if count == 64:
                value = dot(planes_ref[pl.ds(r, m_rows), 512 * b : 512 * b + 256], perm_ref[512:768, :256])
                width = 256
            else:
                value = dot(planes_ref[pl.ds(r, m_rows), 512 * b : 512 * b + 512], perm_ref[:512, :])
                width = 4 * count
            value = value[:, :width]
            scale = scales_ref[i, :, 512 * b : 512 * b + width]
            factor = (1 << (scale - 118)).astype(F32) * (2.0**-10)
            factor = jnp.broadcast_to(factor[:, None, :], (m_rows // 32, 32, width)).reshape(m_rows, width)
            out_ref[pl.ds(r, m_rows), 512 * b : 512 * b + width] = (value * factor).astype(BF16)
        return 0

    lax.fori_loop(0, rows // m_rows, product_step, 0)


def moe_kernel(
    branch_ref, normed_ref, routes_ref, gates_ref, routes_t_ref, gc_hbm, uc_hbm, dc_hbm, gs_hbm, us_hbm, ds_hbm,
    out_ref,
    gc, uc, dc, gs, us, ds, planes, perm, wg, wu, wd,
    send, mine, other, p_mine, p_other, p_in, result, ret,
    in_sem, send_sem, mine_sem, fwd_sem, other_sem, pout_sem, pin_sem, res_sem, ret_sem,
):
    me = lax.axis_index("exp")
    core = me & 1
    z = (me >> 1) & 7
    x_hi = me >> 4

    def peer(i):
        dx, dz = OFFSETS[i]
        return {"exp": (((x_hi + dx) & 1) * 8 + ((z + dz + 8) & 7)) * 2 + core}

    def source(i):
        dx, dz = OFFSETS[i]
        return {"exp": (((x_hi + dx) & 1) * 8 + ((z - dz + 8) & 7)) * 2 + core}

    partner = {"exp": me ^ 1}

    loads = []
    for n, (src, dst) in enumerate(((gc_hbm, gc), (uc_hbm, uc), (dc_hbm, dc), (gs_hbm, gs), (us_hbm, us), (ds_hbm, ds))):
        copy = pltpu.make_async_copy(src, dst, in_sem.at[n])
        copy.start()
        loads.append(copy)

    barrier = pltpu.get_barrier_semaphore()
    for i in range(1, CHIPS):
        pl.semaphore_signal(barrier, inc=1, device_id=peer(i), device_id_type=MESH)
    pl.semaphore_signal(barrier, inc=1, device_id=partner, device_id_type=MESH)

    routes_t = routes_t_ref[...]
    expert = offset_expert(iota((CHIPS, TOK), 0), x_hi, z)
    hit = jnp.zeros((CHIPS, TOK), F32)
    for k in range(TOPK):
        hit = hit + (routes_t[k : k + 1, :] == expert).astype(F32)
    before = (iota((TOK, 256), 0) < (iota((TOK, 256), 1) & 63)).astype(BF16)
    same = (iota((TOK, 256), 0) == (iota((TOK, 256), 1) & 63)).astype(BF16)
    hit16 = hit.astype(BF16)
    slot4 = dot(hit16, before)
    hit4 = dot(hit16, same)
    slot4 = jnp.where(hit4 > 0.5, slot4, -1000.0)
    slot_i = slot4.astype(jnp.int32)
    slot_main = slot_i[:, :TOK]
    pick = (jnp.broadcast_to(slot_main[:, None, :], (CHIPS, 16, TOK)) == iota((CHIPS, 16, TOK), 1)).astype(F32)
    pick = pick.astype(BF16).reshape(CHIPS * 16, TOK)
    rows = dot(pick, normed_ref[...]).astype(BF16)
    for j in range(12):
        send[:, 16 * j : 16 * j + 16, :] = rows[:, 128 * j : 128 * j + 128].reshape(CHIPS, 16, 128)
    tail_key = jnp.where(slot_i >= 16, slot_i - 16 + 4 * (iota((CHIPS, 256), 1) >> 6), -1)
    tail = (jnp.broadcast_to(tail_key[:, None, :], (CHIPS, 16, 256)) == iota((CHIPS, 16, 256), 1)).astype(F32)
    tail = tail.astype(BF16).reshape(CHIPS * 16, 256)
    for g in range(3):
        stacked = jnp.concatenate([normed_ref[:, 128 * (4 * g + j) : 128 * (4 * g + j + 1)] for j in range(4)], axis=0)
        send[:, 192 + 16 * g : 208 + 16 * g, :] = dot(tail, stacked).astype(BF16).reshape(CHIPS, 16, 128)

    pl.semaphore_wait(barrier, CHIPS)

    outgoing = []
    for i in range(1, CHIPS):
        copy = pltpu.make_async_remote_copy(
            src_ref=send.at[i], dst_ref=mine.at[i], send_sem=send_sem.at[i], recv_sem=mine_sem.at[i],
            device_id=peer(i), device_id_type=MESH)
        copy.start()
        outgoing.append(copy)

    def forward(i):
        copy = pltpu.make_async_remote_copy(
            src_ref=send.at[0] if i == 0 else mine.at[i], dst_ref=other.at[i],
            send_sem=fwd_sem.at[i], recv_sem=other_sem.at[i],
            device_id=partner, device_id_type=MESH)
        copy.start()
        return copy

    forwards = [forward(0)]

    expert_of = offset_expert(iota((TOK, CHIPS), 1), x_hi, z)
    routes = routes_ref[...]
    gates = gates_ref[...]
    hits = jnp.zeros((TOK, CHIPS), F32)
    for k in range(TOPK):
        hits = hits + (routes[:, k : k + 1] == expert_of).astype(F32)
    earlier = (iota((TOK, TOK), 1) < iota((TOK, TOK), 0)).astype(BF16)
    slots = jnp.where(hits > 0.5, dot(earlier, hits.astype(BF16)), 100.0)
    spread = (iota((CHIPS, 256), 0) == (iota((CHIPS, 256), 1) >> 4)).astype(BF16)
    slots = dot(slots.astype(BF16), spread).astype(jnp.int32)
    column_expert = offset_expert(iota((TOK, 256), 1) >> 4, x_hi, z)
    weight = jnp.zeros((TOK, 256), F32)
    for k in range(TOPK):
        weight = weight + jnp.where(routes[:, k : k + 1] == column_expert, gates[:, k : k + 1], 0.0)
    place = iota((TOK, 256), 1) & 15
    combine_main = jnp.concatenate(split3(jnp.where(slots == place, weight, 0.0)), axis=0)
    combine_tail = [
        jnp.concatenate(split3(jnp.where((slots - 16 == (place & 3)) & ((place >> 2) == j), weight, 0.0)), axis=0)
        for j in range(4)
    ]

    wide = iota((512, 512), 0)
    perm[:512, :] = (iota((512, 512), 1) == 4 * (wide & 127) + (wide >> 7)).astype(F32).astype(BF16)
    narrow = iota((256, 512), 0)
    perm[512:768, :] = (iota((256, 512), 1) == 4 * (narrow & 63) + (narrow >> 6)).astype(F32).astype(BF16)
    wg[D:, :] = jnp.zeros((DP - D, FF), BF16)
    wu[D:, :] = jnp.zeros((DP - D, FF), BF16)
    wd[:, D:] = jnp.zeros((FF, DP - D), BF16)
    for copy in loads:
        copy.wait()
    decode(gc, gs, planes, perm, wg, D, 192, 288)
    decode(uc, us, planes, perm, wu, D, 192, 288)
    decode(dc, ds, planes, perm, wd, FF, 360, 256)

    a, b = iota((128, 128), 0), iota((128, 128), 1)
    to_rows = (b == ((a >> 2) & 7) * 16 + (a >> 5) * 4 + (a & 3)).astype(F32).astype(BF16)
    to_block = (a == ((b >> 2) & 7) * 16 + (b >> 5) * 4 + (b & 3)).astype(F32).astype(BF16)

    sent_pieces = []
    sent_results = []

    def finish(c):
        sent_pieces[c].wait_recv()
        for i in range(4 * c, 4 * c + 4):
            total = (p_mine[i].astype(F32) + p_in[i].astype(F32)).astype(BF16)
            if i == 0:
                ret[0] = total
            else:
                result[i] = total
        for i in range(max(1, 4 * c), 4 * c + 4):
            copy = pltpu.make_async_remote_copy(
                src_ref=result.at[i], dst_ref=ret.at[i], send_sem=res_sem.at[i], recv_sem=ret_sem.at[i],
                device_id=source(i), device_id_type=MESH)
            copy.start()
            sent_results.append(copy)

    for c in range(4):
        for i in range(max(1, 4 * c), 4 * c + 4):
            outgoing[i - 1].wait_recv()
            forwards.append(forward(i))
        for i in range(4 * c, 4 * c + 4):
            forwards[i].wait_recv()
        if c == 0:
            mine[0] = send[0]

        def both(lo, hi):
            return jnp.concatenate(
                [mine[4 * c : 4 * c + 4, lo:hi, :].reshape(64, 128), other[4 * c : 4 * c + 4, lo:hi, :].reshape(64, 128)],
                axis=0)

        main = jnp.concatenate([both(16 * j, 16 * j + 16) for j in range(12)], axis=1)
        tails = []
        for g in range(3):
            moved = dot(to_rows, both(192 + 16 * g, 208 + 16 * g)).astype(BF16)
            tails += [moved[32 * j : 32 * j + 32, :] for j in range(4)]
        x = jnp.concatenate([main, jnp.concatenate(tails, axis=1)], axis=0)
        gate_act = dot(x, wg[...])
        up_act = dot(x, wu[...])
        active = ((up_act + 1.0) * gate_act * jax.nn.sigmoid(1.702 * gate_act)).astype(BF16)
        y = dot(active, wd[...]).astype(BF16)
        for j in range(12):
            tile = y[:128, 128 * j : 128 * j + 128]
            p_mine[4 * c : 4 * c + 4, 16 * j : 16 * j + 16, :] = tile[:64].reshape(4, 16, 128)
            p_other[4 * c : 4 * c + 4, 16 * j : 16 * j + 16, :] = tile[64:].reshape(4, 16, 128)
        for g in range(3):
            tiles = jnp.concatenate([y[128:, 128 * (4 * g + j) : 128 * (4 * g + j + 1)] for j in range(4)], axis=0)
            back = dot(to_block, tiles).astype(BF16)
            p_mine[4 * c : 4 * c + 4, 192 + 16 * g : 208 + 16 * g, :] = back[:64].reshape(4, 16, 128)
            p_other[4 * c : 4 * c + 4, 192 + 16 * g : 208 + 16 * g, :] = back[64:].reshape(4, 16, 128)
        copy = pltpu.make_async_remote_copy(
            src_ref=p_other.at[pl.ds(4 * c, 4)], dst_ref=p_in.at[pl.ds(4 * c, 4)],
            send_sem=pout_sem.at[c], recv_sem=pin_sem.at[c], device_id=partner, device_id_type=MESH)
        copy.start()
        sent_pieces.append(copy)
        if c > 0:
            finish(c - 1)
    finish(3)

    for copy in sent_results:
        copy.wait_recv()
    for j in range(12):
        part = dot(combine_main, ret[:, 16 * j : 16 * j + 16, :].reshape(256, 128))
        g = j // 4
        part = part + dot(combine_tail[j % 4], ret[:, 192 + 16 * g : 208 + 16 * g, :].reshape(256, 128))
        mixed = part[:TOK] + part[TOK : 2 * TOK] + part[2 * TOK :]
        lo, hi = 128 * j, min(128 * j + 128, D)
        out_ref[:, lo:hi] = (branch_ref[:, lo:hi] + mixed[:, : hi - lo]).astype(BF16)

    for copy in outgoing + forwards + sent_pieces + sent_results:
        copy.wait_send()


def moe(branch, normed, routes, gates, gate_codes, up_codes, down_codes, gate_scales, up_scales, down_scales):
    vmem = pl.BlockSpec(memory_space=pltpu.VMEM)
    hbm = pl.BlockSpec(memory_space=pl.ANY)
    dma = pltpu.SemaphoreType.DMA
    blocks = pltpu.VMEM((CHIPS, BLK, 128), BF16)
    return pl.pallas_call(
        moe_kernel,
        out_shape=jax.ShapeDtypeStruct((TOK, D), BF16),
        in_specs=[vmem] * 5 + [hbm] * 6,
        out_specs=vmem,
        scratch_shapes=[
            pltpu.VMEM((D, 192), jnp.int32),
            pltpu.VMEM((D, 192), jnp.int32),
            pltpu.VMEM((FF, 360), jnp.int32),
            pltpu.VMEM((5, 9, FF), jnp.int32),
            pltpu.VMEM((5, 9, FF), jnp.int32),
            pltpu.VMEM((3, 8, D), jnp.int32),
            pltpu.VMEM((D, DP), BF16),
            pltpu.VMEM((FF, 512), BF16),
            pltpu.VMEM((DP, FF), BF16),
            pltpu.VMEM((DP, FF), BF16),
            pltpu.VMEM((FF, DP), BF16),
            blocks, blocks, blocks, blocks, blocks, blocks, blocks, blocks,
            dma((6,)), dma((CHIPS,)), dma((CHIPS,)), dma((CHIPS,)), dma((CHIPS,)), dma((4,)), dma((4,)),
            dma((CHIPS,)), dma((CHIPS,)),
        ],
        compiler_params=pltpu.CompilerParams(collective_id=0, has_side_effects=True, vmem_limit_bytes=60 * 1024 * 1024),
        name="experts",
    )(
        branch, normed, routes, gates, routes.T, gate_codes, up_codes, down_codes,
        gate_scales.reshape(5, 9, FF), up_scales.reshape(5, 9, FF), down_scales.reshape(3, 8, D),
    )


def attend(local_queries, offset, key_all, value_all, sinks):
    row_count = local_queries.shape[0]
    groups = QH // KVH
    scale = 1.0 / math.sqrt(HD)
    grouped = local_queries.reshape(row_count, KVH, groups, HD)
    key_heads = key_all.reshape(-1, KVH, HD)
    value_heads = value_all.reshape(-1, KVH, HD)
    key_span = 128
    positions = offset + jnp.arange(row_count, dtype=jnp.int32)
    sink_init = jnp.broadcast_to(sinks.reshape(KVH, 1, groups), (KVH, row_count, groups))
    start_state = (
        sink_init,
        jnp.ones_like(sink_init),
        jnp.zeros((KVH, row_count, groups, HD), jnp.float32),
    )

    def advance(block_index, carry):
        run_max, total_sum, numerator = carry
        key_start = block_index * key_span
        key_block = lax.dynamic_slice_in_dim(key_heads, key_start, key_span, 0)
        value_block = lax.dynamic_slice_in_dim(value_heads, key_start, key_span, 0)
        scores = (
            jnp.einsum("nhsd,khd->hnsk", grouped, key_block, preferred_element_type=jnp.float32)
            * scale
        )
        key_pos = key_start + jnp.arange(key_span, dtype=jnp.int32)
        allowed = key_pos[None, None, None, :] <= positions[None, :, None, None]
        scores = jnp.where(allowed, scores, -1e30)
        new_max = jnp.maximum(run_max, jnp.max(scores, axis=-1))
        weights = jnp.exp(scores - new_max[..., None])
        shrink = jnp.exp(run_max - new_max)
        total_sum = total_sum * shrink + jnp.sum(weights, axis=-1)
        numerator = numerator * shrink[..., None] + jnp.einsum(
            "hnsk,khd->hnsd",
            weights.astype(jnp.bfloat16),
            value_block,
            preferred_element_type=jnp.float32,
        )
        return (new_max, total_sum, numerator)

    blocks = (offset + row_count + key_span - 1) // key_span
    run_max, total_sum, numerator = lax.fori_loop(0, blocks, advance, start_state)
    result = numerator / total_sum[..., None]
    return jnp.transpose(result, (1, 0, 2, 3)).reshape(row_count, QH * HD).astype(jnp.bfloat16)


def local(
    queries,
    keys,
    values,
    sinks,
    out_weight,
    norm_gain,
    routes,
    gates,
    gate_codes,
    up_codes,
    down_codes,
    gate_scales,
    up_scales,
    down_scales,
):
    tokens = queries.shape[1]
    ctx_rank = lax.axis_index("ctx")
    key_all, value_all = (
        lax.all_gather(keys[0], "ctx", axis=0, tiled=True),
        lax.all_gather(values[0], "ctx", axis=0, tiled=True),
    )
    local_q = queries[0]
    attended = attend(local_q, ctx_rank * tokens, key_all, value_all, sinks)
    width = out_weight.shape[1]
    branch = jnp.dot(
        attended,
        lax.all_gather(out_weight, "exp", axis=0, tiled=True),
        preferred_element_type=jnp.float32,
    )
    mean_sq = jnp.mean(branch * branch, axis=-1, keepdims=True)
    normed = (branch * lax.rsqrt(mean_sq + 1e-05) * norm_gain).astype(jnp.bfloat16)
    normed = jnp.pad(normed, ((0, 0), (0, DP - D)))
    return moe(
        branch, normed, routes[0], gates[0], gate_codes[0], up_codes[0], down_codes[0],
        gate_scales[0], up_scales[0], down_scales[0],
    )[None]


def solution(mesh):
    return jax.shard_map(
        local,
        mesh=mesh,
        in_specs=(
            P("exp", "ctx", None),
            P("exp", "ctx", None),
            P("exp", "ctx", None),
            P(),
            P("exp", None),
            P(),
            P("exp", "ctx", None),
            P("exp", "ctx", None),
            P("exp", None, None),
            P("exp", None, None),
            P("exp", None, None),
            P("exp", None, None),
            P("exp", None, None),
            P("exp", None, None),
        ),
        out_specs=P("exp", "ctx", None),
        check_vma=False,
    )
```

```python
import functools
import math

import jax
import jax.numpy as jnp
from jax import lax
from jax.experimental import pallas as pl
from jax.experimental.pallas import tpu as pltpu
from jax.sharding import PartitionSpec as P

QH = 32
KVH = 4
HD = 64
TOPK = 4
D = 1440
DP = 1536
FF = 768
TOK = 64
CHIPS = 16
BLK = 240
MESH = pl.DeviceIdType.MESH
F32 = jnp.float32
BF16 = jnp.bfloat16

OFFSETS = []
for step in range(8):
    half = (step + 1) // 2
    dz = half if step % 2 else -half
    OFFSETS += [(0, dz), (1, dz)]


def iota(shape, axis):
    return lax.broadcasted_iota(jnp.int32, shape, axis)


def dot(a, b):
    return jnp.dot(a, b, preferred_element_type=F32)


def offset_expert(i, x_hi, z):
    step = i >> 1
    half = (step + 1) >> 1
    dz = jnp.where((step & 1) == 1, half, -half)
    return ((x_hi + (i & 1)) & 1) * 8 + ((z + dz + 8) & 7)


def split3(x):
    hi = x.astype(BF16)
    rest = x - hi.astype(F32)
    mid = rest.astype(BF16)
    low = (rest - mid.astype(F32)).astype(BF16)
    return hi, mid, low


def fp4_plane(words, shift):
    code = (words >> shift) & 15
    size = code & 7
    twice = size + jnp.maximum(size - 4, 0) + 2 * jnp.maximum(size - 6, 0)
    return jnp.where(code >= 8, -twice, twice).astype(F32).astype(BF16)


def turn(source_ref, target_ref, rows, words):
    for lo in range(0, rows, 128):
        hi = min(lo + 128, rows)
        target_ref[lo:hi, :] = jnp.transpose(source_ref[:, lo:hi])


def code_planes(codes_ref, planes_ref, rows, words):
    blocks = [(b, 128 * b, min(128, words - 128 * b)) for b in range((words + 127) // 128)]

    def step(i, _):
        r = pl.multiple_of(i * 32, 32)
        for b, lo, count in blocks:
            w = codes_ref[pl.ds(r, 32), lo : lo + count]
            if count == 64:
                w = jnp.concatenate([w, w], axis=1)
                shifts = [(iota((32, 128), 1) >> 6) * 4 + 8 * k for k in range(2)]
            else:
                if count < 128:
                    w = jnp.concatenate([w, jnp.zeros((32, 128 - count), jnp.int32)], axis=1)
                shifts = [4 * k for k in range(4)]
            for k, shift in enumerate(shifts):
                at = 512 * b + 128 * k
                planes_ref[pl.ds(r, 32), at : at + 128] = fp4_plane(w, shift)
        return 0

    lax.fori_loop(0, rows // 32, step, 0)


def weight_rows(planes_ref, scales_ref, perm_ref, out_ref, rows, words, m_rows):
    groups = m_rows // 32
    blocks = [(b, min(128, words - 128 * b)) for b in range((words + 127) // 128)]
    for i in range(rows // m_rows):
        r = i * m_rows
        for b, count in blocks:
            width = 4 * count
            if count == 64:
                value = dot(planes_ref[r : r + m_rows, 512 * b : 512 * b + 256], perm_ref[512:768, :256])
            else:
                value = dot(planes_ref[r : r + m_rows, 512 * b : 512 * b + 512], perm_ref[:512, :])
            value = value[:, :width]
            scale = scales_ref[groups * i : groups * (i + 1), 512 * b : 512 * b + width]
            factor = (1 << (scale - 118)).astype(F32) * (2.0**-10)
            for n in range(groups):
                piece = value[32 * n : 32 * n + 32] * factor[n : n + 1]
                out_ref[r + 32 * n : r + 32 * n + 32, 512 * b : 512 * b + width] = piece.astype(BF16)


class Gather:
    RELAYS = {
        ("A", 1): "+", ("A", 2): "+s", ("A", 3): "+s", ("A", 4): "s",
        ("A", -1): "-", ("A", -2): "-", ("A", -3): "s",
        ("B", 0): "+-", ("B", -1): "-",
    }

    def __init__(self, buf, index, sends, recvs, there, partner=None, share=None):
        self.buf, self.index, self.sends, self.recvs = buf, index, sends, recvs
        self.there, self.partner, self.share = there, partner, share
        self.count = 0
        self.waits = {}
        self.copies = []
        self.shared = []

    def send(self, way, side, step):
        where = self.index(side, step)
        if way == "+":
            name = (side, step + 1)
        elif way == "-":
            name = (side, step - 1)
        else:
            name = ("B", step)
        copy = pltpu.make_async_remote_copy(
            src_ref=self.buf.at[where], dst_ref=self.buf.at[where], send_sem=self.sends.at[self.count],
            recv_sem=self.recvs.at[self.count], device_id=self.there[way], device_id_type=MESH)
        copy.start()
        self.count += 1
        self.copies.append(copy)
        self.waits[name] = copy

    def give(self, side, step):
        if self.share is None:
            return
        where = self.index(side, step)
        n = len(self.shared)
        copy = pltpu.make_async_remote_copy(
            src_ref=self.buf.at[where], dst_ref=self.buf.at[where], send_sem=self.share[0].at[n],
            recv_sem=self.share[1].at[n], device_id=self.partner, device_id_type=MESH)
        copy.start()
        self.shared.append(copy)

    def begin(self):
        for way in "+-s":
            self.send(way, "A", 0)
        self.give("A", 0)

    def take(self, side, step):
        self.waits[side, step].wait_recv()
        for way in self.RELAYS.get((side, step), ""):
            self.send(way, side, step)
        self.give(side, step)


def layer_kernel(
    queries_hbm, keys_hbm, values_hbm, sinks_ref, ow_hbm, gain_ref, routes_t_ref, gates_t_ref,
    gc_hbm, uc_hbm, dc_hbm, gs, us, ds,
    out_ref,
    q_in, kv, qz, bias, sink_rows, heads, wbuf, branch_ref, normed_ref,
    gct, uct, dct, gc, uc, dc, planes, perm, wg, wu, wd,
    send, mine, other, p_mine, p_other, p_in, result, ret,
    in_sem, kv_send, kv_recv, ow_send, ow_recv, give_send, give_recv,
    send_sem, mine_sem, fwd_sem, other_sem, pout_sem, pin_sem, res_sem, ret_sem,
):
    me = lax.axis_index("exp")
    ctx = lax.axis_index("ctx")
    core = me & 1
    z = (me >> 1) & 7
    x_hi = me >> 4
    y = ctx >> 1
    x_lo = ctx & 1

    def peer(i):
        dx, dz = OFFSETS[i]
        return {"exp": (((x_hi + dx) & 1) * 8 + ((z + dz + 8) & 7)) * 2 + core}

    def source(i):
        dx, dz = OFFSETS[i]
        return {"exp": (((x_hi + dx) & 1) * 8 + ((z - dz + 8) & 7)) * 2 + core}

    partner = {"exp": me ^ 1}
    kv_there = {
        "+": {"ctx": ((y + 1) & 7) * 2 + x_lo}, "-": {"ctx": ((y + 7) & 7) * 2 + x_lo}, "s": {"ctx": ctx ^ 1},
    }
    ow_there = {
        "+": {"exp": (x_hi * 8 + ((z + 1) & 7)) * 2 + core}, "-": {"exp": (x_hi * 8 + ((z + 7) & 7)) * 2 + core},
        "s": {"ctx": ctx ^ 1, "exp": me ^ 16},
    }

    def kv_index(side, step):
        return ((y - step + 8) & 7) * 2 + (x_lo if side == "A" else 1 - x_lo)

    def ow_index(side, step):
        return ((x_hi if side == "A" else 1 - x_hi) * 8 + ((z - step + 8) & 7)) * 2 + core

    kv_gather = Gather(kv, kv_index, kv_send, kv_recv, kv_there)
    ow_gather = Gather(wbuf, ow_index, ow_send, ow_recv, ow_there, partner, (give_send, give_recv))

    barrier = pltpu.get_barrier_semaphore()
    greeted = [peer(i) for i in range(1, CHIPS)] + [partner, kv_there["+"], kv_there["-"], kv_there["s"], ow_there["s"]]
    for device in greeted:
        pl.semaphore_signal(barrier, inc=1, device_id=device, device_id_type=MESH)

    loads = []
    for n, (src, dst) in enumerate((
        (keys_hbm, kv.at[ctx, :, 0:256]), (values_hbm, kv.at[ctx, :, 256:512]), (ow_hbm, wbuf.at[me]),
        (gc_hbm, gct), (uc_hbm, uct), (dc_hbm, dct), (queries_hbm, q_in),
    )):
        copy = pltpu.make_async_copy(src, dst, in_sem.at[n])
        copy.start()
        loads.append(copy)
    loads[0].wait()
    loads[1].wait()
    loads[2].wait()
    pl.semaphore_wait(barrier, len(greeted))
    kv_gather.begin()
    ow_gather.begin()

    wide = iota((512, 512), 0)
    perm[:512, :] = (iota((512, 512), 1) == 4 * (wide & 127) + (wide >> 7)).astype(F32).astype(BF16)
    narrow = iota((256, 512), 0)
    perm[512:768, :] = (iota((256, 512), 1) == 4 * (narrow & 63) + (narrow >> 6)).astype(F32).astype(BF16)
    wg[D:, :] = jnp.zeros((DP - D, FF), BF16)
    wu[D:, :] = jnp.zeros((DP - D, FF), BF16)
    wd[:, D:] = jnp.zeros((FF, DP - D), BF16)
    normed_ref[:, D:] = jnp.zeros((TOK, DP - D), BF16)
    loads[3].wait()
    turn(gct, gc, D, 192)
    for name in (("A", 1), ("A", -1), ("B", 0)):
        kv_gather.take(*name)
    code_planes(gc, planes, D, 192)
    for name in (("A", 1), ("A", -1), ("B", 0)):
        ow_gather.take(*name)
    for name in (("A", 2), ("A", -2), ("B", -1)):
        kv_gather.take(*name)
    weight_rows(planes, gs, perm, wg, D, 192, 288)
    for name in (("A", 3), ("A", -3)):
        kv_gather.take(*name)
    loads[4].wait()
    turn(uct, uc, D, 192)
    code_planes(uc, planes, D, 192)
    for name in (("A", 2), ("A", -2), ("B", -1)):
        ow_gather.take(*name)
    kv_gather.take("A", 4)
    weight_rows(planes, us, perm, wu, D, 192, 288)

    loads[6].wait()
    left = iota((TOK, 128), 1) < 64
    for h in range(QH):
        g = h // 8
        tile = q_in[:, 128 * (h // 2) : 128 * (h // 2) + 128].astype(F32) * (1.0 / math.sqrt(HD))
        if h % 2 != g % 2:
            tile = pltpu.roll(tile, 64, 1)
        tile = jnp.where(left if g % 2 == 0 else ~left, tile, 0.0).astype(BF16)
        lo = 128 * (g // 2)
        qz[64 * h : 64 * h + 64, lo : lo + 128] = tile
        qz[64 * h : 64 * h + 64, 128 - lo : 256 - lo] = jnp.zeros((TOK, 128), BF16)
        sink_rows[64 * h : 64 * h + 64, :] = jnp.broadcast_to(sinks_ref[h], (TOK, 128))
    bias[...] = jnp.where(iota((TOK, 1024), 1) <= ctx * TOK + iota((TOK, 1024), 0), 0.0, -1e30)

    for name in (("A", 3), ("A", -3)):
        ow_gather.take(*name)
    loads[5].wait()
    turn(dct, dc, FF, 360)
    code_planes(dc, planes, FF, 360)
    for name in (("B", 1), ("B", -2), ("B", 2), ("B", 3), ("B", -3), ("B", 4)):
        kv_gather.take(*name)

    def attend(i, _):
        r = pl.multiple_of(i * 256, 256)
        scores = lax.dot_general(
            qz[pl.ds(r, 256), :], kv[:, :, 0:256].reshape(1024, 256), (((1,), (1,)), ((), ())),
            preferred_element_type=F32)
        scores = (scores.reshape(4, TOK, 1024) + bias[...][None]).reshape(256, 1024)
        sink = sink_rows[pl.ds(r, 256), :1]
        top = jnp.maximum(jnp.max(scores, axis=1, keepdims=True), sink)
        prob = jnp.exp(scores - top)
        total = jnp.exp(sink - top) + jnp.sum(prob, axis=1, keepdims=True)
        heads[pl.ds(r, 256), :] = dot(prob.astype(BF16), kv[:, :, 256:512].reshape(1024, 256)) / total
        return 0

    lax.fori_loop(0, 4, attend, 0)
    ow_gather.take("A", 4)
    lax.fori_loop(4, 8, attend, 0)
    for name in (("B", 1), ("B", -2), ("B", 2), ("B", 3), ("B", -3), ("B", 4)):
        ow_gather.take(*name)

    tiles = []
    for m in range(QH // 2):
        g = m // 4
        pair = []
        for h in (2 * m, 2 * m + 1):
            tile = heads[64 * h : 64 * h + 64, 128 * (g // 2) : 128 * (g // 2) + 128]
            pair.append(pltpu.roll(tile, 64, 1) if h % 2 != g % 2 else tile)
        tiles.append(jnp.where(left, pair[0], pair[1]).astype(BF16))
    attended = jnp.concatenate(tiles, axis=1)
    for copy in ow_gather.shared:
        copy.wait_recv()
    branch = dot(attended, wbuf[...].reshape(QH * HD, D))
    branch_ref[...] = branch
    mean_sq = jnp.sum(branch * branch, axis=1, keepdims=True) * (1.0 / D)
    normed_ref[:, :D] = (branch * lax.rsqrt(mean_sq + 1e-05) * gain_ref[...].reshape(1, D)).astype(BF16)

    routes_t = routes_t_ref[...]
    expert = offset_expert(iota((CHIPS, TOK), 0), x_hi, z)
    hit = jnp.zeros((CHIPS, TOK), F32)
    for k in range(TOPK):
        hit = hit + (routes_t[k : k + 1, :] == expert).astype(F32)
    before = (iota((TOK, 256), 0) < (iota((TOK, 256), 1) & 63)).astype(BF16)
    same = (iota((TOK, 256), 0) == (iota((TOK, 256), 1) & 63)).astype(BF16)
    hit16 = hit.astype(BF16)
    slot4 = dot(hit16, before)
    hit4 = dot(hit16, same)
    slot4 = jnp.where(hit4 > 0.5, slot4, -1000.0)
    slot_i = slot4.astype(jnp.int32)
    slot_main = slot_i[:, :TOK]
    pick = (jnp.broadcast_to(slot_main[:, None, :], (CHIPS, 16, TOK)) == iota((CHIPS, 16, TOK), 1)).astype(F32)
    pick = pick.astype(BF16).reshape(CHIPS * 16, TOK)
    rows = dot(pick, normed_ref[...]).astype(BF16)
    for j in range(12):
        send[:, 16 * j : 16 * j + 16, :] = rows[:, 128 * j : 128 * j + 128].reshape(CHIPS, 16, 128)
    tail_key = jnp.where(slot_i >= 16, slot_i - 16 + 4 * (iota((CHIPS, 256), 1) >> 6), -1)
    tail = (jnp.broadcast_to(tail_key[:, None, :], (CHIPS, 16, 256)) == iota((CHIPS, 16, 256), 1)).astype(F32)
    tail = tail.astype(BF16).reshape(CHIPS * 16, 256)
    for g in range(3):
        stacked = jnp.concatenate([normed_ref[:, 128 * (4 * g + j) : 128 * (4 * g + j + 1)] for j in range(4)], axis=0)
        send[:, 192 + 16 * g : 208 + 16 * g, :] = dot(tail, stacked).astype(BF16).reshape(CHIPS, 16, 128)

    outgoing = []
    for i in range(1, CHIPS):
        copy = pltpu.make_async_remote_copy(
            src_ref=send.at[i], dst_ref=mine.at[i], send_sem=send_sem.at[i], recv_sem=mine_sem.at[i],
            device_id=peer(i), device_id_type=MESH)
        copy.start()
        outgoing.append(copy)

    def forward(i):
        copy = pltpu.make_async_remote_copy(
            src_ref=send.at[0] if i == 0 else mine.at[i], dst_ref=other.at[i],
            send_sem=fwd_sem.at[i], recv_sem=other_sem.at[i],
            device_id=partner, device_id_type=MESH)
        copy.start()
        return copy

    forwards = [forward(0)]

    padded = jnp.concatenate(
        [routes_t.astype(F32), gates_t_ref[...]], axis=0)
    padded = jnp.transpose(jnp.concatenate([padded, jnp.zeros((8, 64), F32)], axis=1))[:TOK, :]
    routes = padded[:, :TOPK].astype(jnp.int32)
    gates = padded[:, TOPK:]
    expert_of = offset_expert(iota((TOK, CHIPS), 1), x_hi, z)
    hits = jnp.zeros((TOK, CHIPS), F32)
    for k in range(TOPK):
        hits = hits + (routes[:, k : k + 1] == expert_of).astype(F32)
    earlier = (iota((TOK, TOK), 1) < iota((TOK, TOK), 0)).astype(BF16)
    slots = jnp.where(hits > 0.5, dot(earlier, hits.astype(BF16)), 100.0)
    spread = (iota((CHIPS, 256), 0) == (iota((CHIPS, 256), 1) >> 4)).astype(BF16)
    slots = dot(slots.astype(BF16), spread).astype(jnp.int32)
    column_expert = offset_expert(iota((TOK, 256), 1) >> 4, x_hi, z)
    weight = jnp.zeros((TOK, 256), F32)
    for k in range(TOPK):
        weight = weight + jnp.where(routes[:, k : k + 1] == column_expert, gates[:, k : k + 1], 0.0)
    place = iota((TOK, 256), 1) & 15
    combine_main = jnp.concatenate(split3(jnp.where(slots == place, weight, 0.0)), axis=0)
    combine_tail = [
        jnp.concatenate(split3(jnp.where((slots - 16 == (place & 3)) & ((place >> 2) == j), weight, 0.0)), axis=0)
        for j in range(4)
    ]

    weight_rows(planes, ds, perm, wd, FF, 360, 256)

    a, b = iota((128, 128), 0), iota((128, 128), 1)
    to_rows = (b == ((a >> 2) & 7) * 16 + (a >> 5) * 4 + (a & 3)).astype(F32).astype(BF16)
    to_block = (a == ((b >> 2) & 7) * 16 + (b >> 5) * 4 + (b & 3)).astype(F32).astype(BF16)

    sent_pieces = []
    sent_results = []

    def finish(c):
        sent_pieces[c].wait_recv()
        for i in range(4 * c, 4 * c + 4):
            total = (p_mine[i].astype(F32) + p_in[i].astype(F32)).astype(BF16)
            if i == 0:
                ret[0] = total
            else:
                result[i] = total
        for i in range(max(1, 4 * c), 4 * c + 4):
            copy = pltpu.make_async_remote_copy(
                src_ref=result.at[i], dst_ref=ret.at[i], send_sem=res_sem.at[i], recv_sem=ret_sem.at[i],
                device_id=source(i), device_id_type=MESH)
            copy.start()
            sent_results.append(copy)

    for c in range(4):
        for i in range(max(1, 4 * c), 4 * c + 4):
            outgoing[i - 1].wait_recv()
            forwards.append(forward(i))
        for i in range(4 * c, 4 * c + 4):
            forwards[i].wait_recv()
        if c == 0:
            mine[0] = send[0]

        def both(lo, hi):
            return jnp.concatenate(
                [mine[4 * c : 4 * c + 4, lo:hi, :].reshape(64, 128), other[4 * c : 4 * c + 4, lo:hi, :].reshape(64, 128)],
                axis=0)

        main = jnp.concatenate([both(16 * j, 16 * j + 16) for j in range(12)], axis=1)
        tails = []
        for g in range(3):
            moved = dot(to_rows, both(192 + 16 * g, 208 + 16 * g)).astype(BF16)
            tails += [moved[32 * j : 32 * j + 32, :] for j in range(4)]
        x = jnp.concatenate([main, jnp.concatenate(tails, axis=1)], axis=0)
        gate_act = dot(x, wg[...])
        up_act = dot(x, wu[...])
        active = ((up_act + 1.0) * gate_act * jax.nn.sigmoid(1.702 * gate_act)).astype(BF16)
        y = dot(active, wd[...]).astype(BF16)
        for j in range(12):
            tile = y[:128, 128 * j : 128 * j + 128]
            p_mine[4 * c : 4 * c + 4, 16 * j : 16 * j + 16, :] = tile[:64].reshape(4, 16, 128)
            p_other[4 * c : 4 * c + 4, 16 * j : 16 * j + 16, :] = tile[64:].reshape(4, 16, 128)
        for g in range(3):
            tiles = jnp.concatenate([y[128:, 128 * (4 * g + j) : 128 * (4 * g + j + 1)] for j in range(4)], axis=0)
            back = dot(to_block, tiles).astype(BF16)
            p_mine[4 * c : 4 * c + 4, 192 + 16 * g : 208 + 16 * g, :] = back[:64].reshape(4, 16, 128)
            p_other[4 * c : 4 * c + 4, 192 + 16 * g : 208 + 16 * g, :] = back[64:].reshape(4, 16, 128)
        copy = pltpu.make_async_remote_copy(
            src_ref=p_other.at[pl.ds(4 * c, 4)], dst_ref=p_in.at[pl.ds(4 * c, 4)],
            send_sem=pout_sem.at[c], recv_sem=pin_sem.at[c], device_id=partner, device_id_type=MESH)
        copy.start()
        sent_pieces.append(copy)
        if c > 0:
            finish(c - 1)
    finish(3)

    for copy in sent_results:
        copy.wait_recv()
    for j in range(12):
        part = dot(combine_main, ret[:, 16 * j : 16 * j + 16, :].reshape(256, 128))
        g = j // 4
        part = part + dot(combine_tail[j % 4], ret[:, 192 + 16 * g : 208 + 16 * g, :].reshape(256, 128))
        mixed = part[:TOK] + part[TOK : 2 * TOK] + part[2 * TOK :]
        lo, hi = 128 * j, min(128 * j + 128, D)
        out_ref[:, lo:hi] = (branch_ref[:, lo:hi] + mixed[:, : hi - lo]).astype(BF16)

    for copy in outgoing + forwards + sent_pieces + sent_results + kv_gather.copies + ow_gather.copies + ow_gather.shared:
        copy.wait_send()


def local(
    queries, keys, values, sinks, out_weight, norm_gain, routes, gates,
    gate_codes, up_codes, down_codes, gate_scales, up_scales, down_scales,
):
    vmem = pl.BlockSpec(memory_space=pltpu.VMEM)
    hbm = pl.BlockSpec(memory_space=pl.ANY)
    dma = pltpu.SemaphoreType.DMA
    blocks = pltpu.VMEM((CHIPS, BLK, 128), BF16)
    out = pl.pallas_call(
        layer_kernel,
        out_shape=jax.ShapeDtypeStruct((TOK, D), BF16),
        in_specs=[hbm] * 3 + [pl.BlockSpec(memory_space=pltpu.SMEM), hbm] + [vmem] * 3 + [hbm] * 3 + [vmem] * 3,
        out_specs=vmem,
        scratch_shapes=[
            pltpu.VMEM((TOK, QH * HD), BF16),
            pltpu.VMEM((16, TOK, 512), BF16),
            pltpu.VMEM((QH * TOK, 256), BF16),
            pltpu.VMEM((TOK, 1024), F32),
            pltpu.VMEM((QH * TOK, 128), F32),
            pltpu.VMEM((QH * TOK, 256), F32),
            pltpu.VMEM((32, 64, D), BF16),
            pltpu.VMEM((TOK, D), F32),
            pltpu.VMEM((TOK, DP), BF16),
            pltpu.VMEM((192, D), jnp.int32),
            pltpu.VMEM((192, D), jnp.int32),
            pltpu.VMEM((360, FF), jnp.int32),
            pltpu.VMEM((D, 192), jnp.int32),
            pltpu.VMEM((D, 192), jnp.int32),
            pltpu.VMEM((FF, 360), jnp.int32),
            pltpu.VMEM((D, DP), BF16),
            pltpu.VMEM((FF, 512), BF16),
            pltpu.VMEM((DP, FF), BF16),
            pltpu.VMEM((DP, FF), BF16),
            pltpu.VMEM((FF, DP), BF16),
            blocks, blocks, blocks, blocks, blocks, blocks, blocks, blocks,
            dma((7,)), dma((15,)), dma((15,)), dma((15,)), dma((15,)), dma((16,)), dma((16,)),
            dma((CHIPS,)), dma((CHIPS,)), dma((CHIPS,)), dma((CHIPS,)), dma((4,)), dma((4,)),
            dma((CHIPS,)), dma((CHIPS,)),
        ],
        compiler_params=pltpu.CompilerParams(collective_id=0, has_side_effects=True, vmem_limit_bytes=60 * 1024 * 1024),
        name="layer",
    )(
        queries[0], keys[0], values[0], sinks, out_weight, norm_gain.reshape(1, D), routes[0].T, gates[0].T,
        gate_codes[0].T, up_codes[0].T, down_codes[0].T, gate_scales[0], up_scales[0], down_scales[0],
    )
    return out[None]


def solution(mesh):
    return jax.shard_map(
        local,
        mesh=mesh,
        in_specs=(
            P("exp", "ctx", None),
            P("exp", "ctx", None),
            P("exp", "ctx", None),
            P(),
            P("exp", None),
            P(),
            P("exp", "ctx", None),
            P("exp", "ctx", None),
            P("exp", None, None),
            P("exp", None, None),
            P("exp", None, None),
            P("exp", None, None),
            P("exp", None, None),
            P("exp", None, None),
        ),
        out_specs=P("exp", "ctx", None),
        check_vma=False,
    )
```

```python
import functools
import math

import jax
import jax.numpy as jnp
from jax import lax
from jax.experimental import pallas as pl
from jax.experimental.pallas import tpu as pltpu
from jax.sharding import PartitionSpec as P

QH = 32
KVH = 4
HD = 64
TOPK = 4
D = 1440
DP = 1536
FF = 768
TOK = 64
CHIPS = 16
BLK = 240
MESH = pl.DeviceIdType.MESH
F32 = jnp.float32
BF16 = jnp.bfloat16

OFFSETS = []
for step in range(8):
    half = (step + 1) // 2
    dz = half if step % 2 else -half
    OFFSETS += [(0, dz), (1, dz)]


def iota(shape, axis):
    return lax.broadcasted_iota(jnp.int32, shape, axis)


def dot(a, b):
    return jnp.dot(a, b, preferred_element_type=F32)


def offset_expert(i, x_hi, z):
    step = i >> 1
    half = (step + 1) >> 1
    dz = jnp.where((step & 1) == 1, half, -half)
    return ((x_hi + (i & 1)) & 1) * 8 + ((z + dz + 8) & 7)


def split3(x):
    hi = x.astype(BF16)
    rest = x - hi.astype(F32)
    mid = rest.astype(BF16)
    low = (rest - mid.astype(F32)).astype(BF16)
    return hi, mid, low


def fp4_plane(words, shift):
    code = (words >> shift) & 15
    size = code & 7
    twice = size + jnp.maximum(size - 4, 0) + 2 * jnp.maximum(size - 6, 0)
    return jnp.where(code >= 8, -twice, twice).astype(F32).astype(BF16)


def turn(source_ref, target_ref, rows, words):
    for lo in range(0, rows, 128):
        hi = min(lo + 128, rows)
        target_ref[lo:hi, :] = jnp.transpose(source_ref[:, lo:hi])


def code_planes(codes_ref, planes_ref, rows, words):
    blocks = [(b, 128 * b, min(128, words - 128 * b)) for b in range((words + 127) // 128)]

    def step(i, _):
        r = pl.multiple_of(i * 32, 32)
        for b, lo, count in blocks:
            w = codes_ref[pl.ds(r, 32), lo : lo + count]
            if count == 64:
                w = jnp.concatenate([w, w], axis=1)
                shifts = [(iota((32, 128), 1) >> 6) * 4 + 8 * k for k in range(2)]
            else:
                if count < 128:
                    w = jnp.concatenate([w, jnp.zeros((32, 128 - count), jnp.int32)], axis=1)
                shifts = [4 * k for k in range(4)]
            for k, shift in enumerate(shifts):
                at = 512 * b + 128 * k
                planes_ref[pl.ds(r, 32), at : at + 128] = fp4_plane(w, shift)
        return 0

    lax.fori_loop(0, rows // 32, step, 0)


def weight_rows(planes_ref, scales_ref, perm_ref, out_ref, rows, words, m_rows):
    groups = m_rows // 32
    blocks = [(b, min(128, words - 128 * b)) for b in range((words + 127) // 128)]
    for i in range(rows // m_rows):
        r = i * m_rows
        for b, count in blocks:
            width = 4 * count
            if count == 64:
                value = dot(planes_ref[r : r + m_rows, 512 * b : 512 * b + 256], perm_ref[512:768, :256])
            else:
                value = dot(planes_ref[r : r + m_rows, 512 * b : 512 * b + 512], perm_ref[:512, :])
            value = value[:, :width]
            scale = scales_ref[groups * i : groups * (i + 1), ..., 512 * b : 512 * b + width]
            factor = (1 << (scale - 118)).astype(F32) * (2.0**-10)
            for n in range(groups):
                piece = value[32 * n : 32 * n + 32] * (factor[n] if factor.ndim == 3 else factor[n : n + 1])
                out_ref[r + 32 * n : r + 32 * n + 32, 512 * b : 512 * b + width] = piece.astype(BF16)


class Gather:
    RELAYS = {
        ("A", 1): "+", ("A", 2): "+s", ("A", 3): "+s", ("A", 4): "s",
        ("A", -1): "-", ("A", -2): "-", ("A", -3): "s",
        ("B", 0): "+-", ("B", -1): "-",
    }

    def __init__(self, buf, index, sends, recvs, there):
        self.buf, self.index, self.sends, self.recvs = buf, index, sends, recvs
        self.there = there
        self.count = 0
        self.waits = {}
        self.copies = []

    def send(self, way, side, step):
        where = self.index(side, step)
        if way == "+":
            name = (side, step + 1)
        elif way == "-":
            name = (side, step - 1)
        else:
            name = ("B", step)
        copy = pltpu.make_async_remote_copy(
            src_ref=self.buf.at[where], dst_ref=self.buf.at[where], send_sem=self.sends.at[self.count],
            recv_sem=self.recvs.at[self.count], device_id=self.there[way], device_id_type=MESH)
        copy.start()
        self.count += 1
        self.copies.append(copy)
        self.waits[name] = copy

    def begin(self):
        for way in "+-s":
            self.send(way, "A", 0)

    def take(self, side, step):
        self.waits[side, step].wait_recv()
        for way in self.RELAYS.get((side, step), ""):
            self.send(way, side, step)


class WeightGather:
    def __init__(self, buf, unit, turn, there, partner, sems):
        self.buf, self.unit, self.sign, self.there, self.partner = buf, unit, turn, there, partner
        self.sends, self.recvs, self.give_sends, self.give_recvs = sems
        self.copies, self.given, self.by_name = [], [], {}

    def send(self, name, way, side, step, half):
        where = self.unit(side, step, half)
        n = len(self.copies)
        copy = pltpu.make_async_remote_copy(
            src_ref=self.buf.at[where], dst_ref=self.buf.at[where], send_sem=self.sends.at[n],
            recv_sem=self.recvs.at[n], device_id=self.there[way], device_id_type=MESH)
        copy.start()
        self.copies.append(copy)
        self.by_name[name + (half,)] = copy

    def give(self, side, step, half):
        where = self.unit(side, step, half)
        n = len(self.given)
        copy = pltpu.make_async_remote_copy(
            src_ref=self.buf.at[where], dst_ref=self.buf.at[where], send_sem=self.give_sends.at[n],
            recv_sem=self.give_recvs.at[n], device_id=self.partner, device_id_type=MESH)
        copy.start()
        self.given.append(copy)

    def begin(self):
        for half in range(2):
            self.send(("A", 1), "+", "A", 0, half)
            self.send(("A", -1), "-", "A", 0, half)
            self.send(("B", 0), "cross", "A", 0, half)
        for half in range(2):
            self.give("A", 0, half)

    def ring(self, k, half):
        ways = [1, -1] if k < 4 else [1 if half == 0 else -1]
        for way in ways:
            self.by_name["A", way * k, half].wait_recv()
        for way in ways:
            if k < 3 or (k == 3 and (half == 0) == (way == 1)):
                self.send(("A", way * (k + 1)), "+" if way == 1 else "-", "A", way * k, half)
        if k < 4:
            self.send(("B", "near", k), "cross", "A", -self.sign * k, half)
        else:
            self.send(("B", 4), "cross", "A", 4, half)
        for way in ways:
            self.give("A", way * k, half)

    def near(self, k, half):
        self.by_name["B", "near", k, half].wait_recv()
        self.send(("B", "far", k), "pair", "B", self.sign * k, half)
        self.give("B", self.sign * k, half)

    def far(self, k, half):
        self.by_name["B", "far", k, half].wait_recv()
        self.give("B", -self.sign * k, half)

    def other(self, k, half):
        self.by_name["B", k, half].wait_recv()
        self.give("B", k, half)


def layer_kernel(
    queries_hbm, keys_hbm, values_hbm, sinks_ref, ow_hbm, gain_ref, routes_t_ref, gates_t_ref,
    gc_hbm, uc_hbm, dc_hbm, gs, us, ds,
    out_ref,
    q_in, kv, qz, tops, totals, heads, wbuf, branch_ref, normed_ref,
    gct, uct, dct, gc, uc, dc, planes, perm, wg, wu, wd,
    send, mine, other, p_mine, p_other, p_in, result, ret,
    in_sem, kv_send, kv_recv, ow_send, ow_recv, give_send, give_recv,
    send_sem, mine_sem, fwd_sem, other_sem, pout_sem, pin_sem, res_sem, ret_sem,
):
    me = lax.axis_index("exp")
    ctx = lax.axis_index("ctx")
    core = me & 1
    z = (me >> 1) & 7
    x_hi = me >> 4
    y = ctx >> 1
    x_lo = ctx & 1

    def peer(i):
        dx, dz = OFFSETS[i]
        return {"exp": (((x_hi + dx) & 1) * 8 + ((z + dz + 8) & 7)) * 2 + core, "ctx": ctx ^ dx}

    def source(i):
        dx, dz = OFFSETS[i]
        return {"exp": (((x_hi + dx) & 1) * 8 + ((z - dz + 8) & 7)) * 2 + core, "ctx": ctx ^ dx}

    partner = {"exp": me ^ 1}
    kv_there = {
        "+": {"ctx": ((y + 1) & 7) * 2 + x_lo}, "-": {"ctx": ((y + 7) & 7) * 2 + x_lo}, "s": {"ctx": ctx ^ 1},
    }
    ow_there = {
        "+": {"exp": (x_hi * 8 + ((z + 1) & 7)) * 2 + core}, "-": {"exp": (x_hi * 8 + ((z + 7) & 7)) * 2 + core},
        "cross": {"ctx": ctx ^ 1, "exp": me ^ 16}, "pair": {"ctx": ctx ^ 1},
    }

    def kv_index(side, step):
        return ((y - step + 8) & 7) * 2 + (x_lo if side == "A" else 1 - x_lo)

    def ow_unit(side, step, half):
        return (((x_hi if side == "A" else 1 - x_hi) * 8 + ((z - step + 8) & 7)) * 2 + core) * 2 + half

    kv_gather = Gather(kv, kv_index, kv_send, kv_recv, kv_there)
    ow_gather = WeightGather(
        wbuf, ow_unit, 1 - 2 * x_lo, ow_there, partner, (ow_send, ow_recv, give_send, give_recv))

    barrier = pltpu.get_barrier_semaphore()
    greeted = [peer(i) for i in range(1, CHIPS)] + [partner, kv_there["+"], kv_there["-"], kv_there["s"]]
    for device in greeted:
        pl.semaphore_signal(barrier, inc=1, device_id=device, device_id_type=MESH)

    loads = []
    for n, (src, dst) in enumerate((
        (keys_hbm, kv.at[ctx, :, 0:256]), (values_hbm, kv.at[ctx, :, 256:512]), (ow_hbm, wbuf.at[pl.ds(2 * me, 2)]),
        (gc_hbm, gct), (uc_hbm, uct), (dc_hbm, dct), (queries_hbm, q_in),
    )):
        copy = pltpu.make_async_copy(src, dst, in_sem.at[n])
        copy.start()
        loads.append(copy)
    loads[0].wait()
    loads[1].wait()
    loads[2].wait()
    pl.semaphore_wait(barrier, len(greeted))
    kv_gather.begin()
    ow_gather.begin()

    loads[6].wait()
    left = iota((TOK, 128), 1) < 64
    for h in range(QH):
        g = h // 8
        tile = q_in[:, 128 * (h // 2) : 128 * (h // 2) + 128].astype(F32) * (1.0 / math.sqrt(HD))
        if h % 2 != g % 2:
            tile = pltpu.roll(tile, 64, 1)
        tile = jnp.where(left if g % 2 == 0 else ~left, tile, 0.0).astype(BF16)
        lo = 128 * (g // 2)
        qz[64 * h : 64 * h + 64, lo : lo + 128] = tile
        qz[64 * h : 64 * h + 64, 128 - lo : 256 - lo] = jnp.zeros((TOK, 128), BF16)
        tops[64 * h : 64 * h + 64, :] = jnp.broadcast_to(sinks_ref[h], (TOK, 128))
    normed_ref[:, D:] = jnp.zeros((TOK, DP - D), BF16)

    def attend(names, part, first=False):
        where = [kv_index(*name) for name in names]
        lane = iota((TOK, 256), 1)
        owner = jnp.where(lane < 128, jnp.where(lane < 64, where[0], where[1]), jnp.where(lane < 192, where[2], where[3]))
        bias = jnp.where(owner * TOK + (lane & 63) <= ctx * TOK + iota((TOK, 256), 0), 0.0, -1e30)

        def rows(i, _):
            r = pl.multiple_of(i * 512, 512)
            key_block = jnp.concatenate([kv[w, :, 0:256] for w in where], axis=0)
            value_block = jnp.concatenate([kv[w, :, 256:512] for w in where], axis=0)
            scores = lax.dot_general(
                qz[pl.ds(r, 512), :], key_block, (((1,), (1,)), ((), ())), preferred_element_type=F32)
            scores = (scores.reshape(8, TOK, 256) + bias[None]).reshape(512, 256)
            old = tops[pl.ds(r, 512), :1]
            top = jnp.maximum(jnp.max(scores, axis=1, keepdims=True), old)
            prob = jnp.exp(scores - top)
            shrink = jnp.exp(old - top)
            added = jnp.sum(prob, axis=1, keepdims=True)
            value = dot(prob.astype(BF16), value_block)
            tops[pl.ds(r, 512), :] = jnp.broadcast_to(top, (512, 128))
            if first:
                totals[pl.ds(r, 512), :] = jnp.broadcast_to(shrink + added, (512, 128))
                heads[pl.ds(r, 512), :] = value
            else:
                totals[pl.ds(r, 512), :] = totals[pl.ds(r, 512), :] * shrink + added
                heads[pl.ds(r, 512), :] = heads[pl.ds(r, 512), :] * shrink + value
            return 0

        lax.fori_loop(2 * part, 2 * part + 2, rows, 0)

    def take(*names):
        for name in names:
            kv_gather.take(*name)

    chunks = [
        (("A", 0), ("A", 1), ("A", -1), ("B", 0)), (("A", 2), ("A", -2), ("B", 1), ("B", -1)),
        (("A", 3), ("A", -3), ("B", 2), ("B", -2)), (("A", 4), ("B", 3), ("B", -3), ("B", 4)),
    ]
    take(*chunks[0][1:])
    ow_gather.ring(1, 0)
    attend(chunks[0], 0, True)
    ow_gather.ring(1, 1)
    take(("A", 2), ("A", -2))
    attend(chunks[0], 1, True)
    take(("B", 1), ("B", -1))
    ow_gather.ring(2, 0)
    take(("A", 3), ("A", -3))
    ow_gather.near(1, 0)
    ow_gather.near(1, 1)
    attend(chunks[1], 0)
    ow_gather.ring(2, 1)
    take(("B", 2), ("B", -2))
    attend(chunks[1], 1)
    take(("A", 4),)
    ow_gather.ring(3, 0)
    ow_gather.near(2, 0)
    attend(chunks[2], 0)
    ow_gather.near(2, 1)
    attend(chunks[2], 1)
    ow_gather.ring(3, 1)
    take(("B", 3), ("B", -3), ("B", 4))
    ow_gather.near(3, 0)
    attend(chunks[3], 0)
    ow_gather.ring(4, 0)
    ow_gather.ring(4, 1)
    attend(chunks[3], 1)
    ow_gather.near(3, 1)
    ow_gather.other(0, 0)
    ow_gather.other(0, 1)
    loads[3].wait()
    turn(gct, gc, D, 192)
    for k in (1, 2):
        for half in range(2):
            ow_gather.far(k, half)

    tiles = []
    for m in range(QH // 2):
        g = m // 4
        pair = []
        for h in (2 * m, 2 * m + 1):
            tile = heads[64 * h : 64 * h + 64, 128 * (g // 2) : 128 * (g // 2) + 128]
            tile = tile / totals[64 * h : 64 * h + 64, :]
            pair.append(pltpu.roll(tile, 64, 1) if h % 2 != g % 2 else tile)
        tiles.append(jnp.where(left, pair[0], pair[1]).astype(BF16))
    attended = jnp.concatenate(tiles, axis=1)
    for half in range(2):
        ow_gather.far(3, half)
        ow_gather.other(4, half)
    for copy in ow_gather.given:
        copy.wait_recv()
    branch = dot(attended, wbuf[...].reshape(QH * HD, D))
    branch_ref[...] = branch
    mean_sq = jnp.sum(branch * branch, axis=1, keepdims=True) * (1.0 / D)
    normed_ref[:, :D] = (branch * lax.rsqrt(mean_sq + 1e-05) * gain_ref[...].reshape(1, D)).astype(BF16)

    routes_t = routes_t_ref[...]
    expert = offset_expert(iota((CHIPS, TOK), 0), x_hi, z)
    hit = jnp.zeros((CHIPS, TOK), F32)
    for k in range(TOPK):
        hit = hit + (routes_t[k : k + 1, :] == expert).astype(F32)
    before = (iota((TOK, 256), 0) < (iota((TOK, 256), 1) & 63)).astype(BF16)
    same = (iota((TOK, 256), 0) == (iota((TOK, 256), 1) & 63)).astype(BF16)
    hit16 = hit.astype(BF16)
    slot4 = dot(hit16, before)
    hit4 = dot(hit16, same)
    slot4 = jnp.where(hit4 > 0.5, slot4, -1000.0)
    slot_i = slot4.astype(jnp.int32)
    slot_main = slot_i[:, :TOK]
    pick = (jnp.broadcast_to(slot_main[:, None, :], (CHIPS, 16, TOK)) == iota((CHIPS, 16, TOK), 1)).astype(F32)
    pick = pick.astype(BF16).reshape(CHIPS * 16, TOK)
    rows = dot(pick, normed_ref[...]).astype(BF16)
    for j in range(12):
        send[:, 16 * j : 16 * j + 16, :] = rows[:, 128 * j : 128 * j + 128].reshape(CHIPS, 16, 128)
    tail_key = jnp.where(slot_i >= 16, slot_i - 16 + 4 * (iota((CHIPS, 256), 1) >> 6), -1)
    tail = (jnp.broadcast_to(tail_key[:, None, :], (CHIPS, 16, 256)) == iota((CHIPS, 16, 256), 1)).astype(F32)
    tail = tail.astype(BF16).reshape(CHIPS * 16, 256)
    for g in range(3):
        stacked = jnp.concatenate([normed_ref[:, 128 * (4 * g + j) : 128 * (4 * g + j + 1)] for j in range(4)], axis=0)
        send[:, 192 + 16 * g : 208 + 16 * g, :] = dot(tail, stacked).astype(BF16).reshape(CHIPS, 16, 128)

    outgoing = []
    for i in range(1, CHIPS):
        copy = pltpu.make_async_remote_copy(
            src_ref=send.at[i], dst_ref=mine.at[i], send_sem=send_sem.at[i], recv_sem=mine_sem.at[i],
            device_id=peer(i), device_id_type=MESH)
        copy.start()
        outgoing.append(copy)

    def forward(i):
        copy = pltpu.make_async_remote_copy(
            src_ref=send.at[0] if i == 0 else mine.at[i], dst_ref=other.at[i],
            send_sem=fwd_sem.at[i], recv_sem=other_sem.at[i],
            device_id=partner, device_id_type=MESH)
        copy.start()
        return copy

    forwards = [forward(0)]

    padded = jnp.concatenate(
        [routes_t.astype(F32), gates_t_ref[...]], axis=0)
    padded = jnp.transpose(jnp.concatenate([padded, jnp.zeros((8, 64), F32)], axis=1))[:TOK, :]
    routes = padded[:, :TOPK].astype(jnp.int32)
    gates = padded[:, TOPK:]
    expert_of = offset_expert(iota((TOK, CHIPS), 1), x_hi, z)
    hits = jnp.zeros((TOK, CHIPS), F32)
    for k in range(TOPK):
        hits = hits + (routes[:, k : k + 1] == expert_of).astype(F32)
    earlier = (iota((TOK, TOK), 1) < iota((TOK, TOK), 0)).astype(BF16)
    slots = jnp.where(hits > 0.5, dot(earlier, hits.astype(BF16)), 100.0)
    spread = (iota((CHIPS, 256), 0) == (iota((CHIPS, 256), 1) >> 4)).astype(BF16)
    slots = dot(slots.astype(BF16), spread).astype(jnp.int32)
    column_expert = offset_expert(iota((TOK, 256), 1) >> 4, x_hi, z)
    weight = jnp.zeros((TOK, 256), F32)
    for k in range(TOPK):
        weight = weight + jnp.where(routes[:, k : k + 1] == column_expert, gates[:, k : k + 1], 0.0)
    place = iota((TOK, 256), 1) & 15
    combine_main = jnp.concatenate(split3(jnp.where(slots == place, weight, 0.0)), axis=0)
    combine_tail = [
        jnp.concatenate(split3(jnp.where((slots - 16 == (place & 3)) & ((place >> 2) == j), weight, 0.0)), axis=0)
        for j in range(4)
    ]

    wide = iota((512, 512), 0)
    perm[:512, :] = (iota((512, 512), 1) == 4 * (wide & 127) + (wide >> 7)).astype(F32).astype(BF16)
    narrow = iota((256, 512), 0)
    perm[512:768, :] = (iota((256, 512), 1) == 4 * (narrow & 63) + (narrow >> 6)).astype(F32).astype(BF16)
    wg[D:, :] = jnp.zeros((DP - D, FF), BF16)
    wu[D:, :] = jnp.zeros((DP - D, FF), BF16)
    wd[:, D:] = jnp.zeros((FF, DP - D), BF16)
    code_planes(gc, planes, D, 192)
    weight_rows(planes, gs, perm, wg, D, 192, 288)
    loads[4].wait()
    turn(uct, uc, D, 192)
    code_planes(uc, planes, D, 192)
    weight_rows(planes, us, perm, wu, D, 192, 288)
    loads[5].wait()
    turn(dct, dc, FF, 360)
    code_planes(dc, planes, FF, 360)
    weight_rows(planes, ds, perm, wd, FF, 360, 256)

    a, b = iota((128, 128), 0), iota((128, 128), 1)
    to_rows = (b == ((a >> 2) & 7) * 16 + (a >> 5) * 4 + (a & 3)).astype(F32).astype(BF16)
    to_block = (a == ((b >> 2) & 7) * 16 + (b >> 5) * 4 + (b & 3)).astype(F32).astype(BF16)

    sent_pieces = []
    sent_results = []

    def finish(c):
        sent_pieces[c].wait_recv()
        for i in range(4 * c, 4 * c + 4):
            total = (p_mine[i].astype(F32) + p_in[i].astype(F32)).astype(BF16)
            if i == 0:
                ret[0] = total
            else:
                result[i] = total
        for i in range(max(1, 4 * c), 4 * c + 4):
            copy = pltpu.make_async_remote_copy(
                src_ref=result.at[i], dst_ref=ret.at[i], send_sem=res_sem.at[i], recv_sem=ret_sem.at[i],
                device_id=source(i), device_id_type=MESH)
            copy.start()
            sent_results.append(copy)

    for c in range(4):
        for i in range(max(1, 4 * c), 4 * c + 4):
            outgoing[i - 1].wait_recv()
            forwards.append(forward(i))
        for i in range(4 * c, 4 * c + 4):
            forwards[i].wait_recv()
        if c == 0:
            mine[0] = send[0]

        def both(lo, hi):
            return jnp.concatenate(
                [mine[4 * c : 4 * c + 4, lo:hi, :].reshape(64, 128), other[4 * c : 4 * c + 4, lo:hi, :].reshape(64, 128)],
                axis=0)

        main = jnp.concatenate([both(16 * j, 16 * j + 16) for j in range(12)], axis=1)
        tails = []
        for g in range(3):
            moved = dot(to_rows, both(192 + 16 * g, 208 + 16 * g)).astype(BF16)
            tails += [moved[32 * j : 32 * j + 32, :] for j in range(4)]
        x = jnp.concatenate([main, jnp.concatenate(tails, axis=1)], axis=0)
        gate_act = dot(x, wg[...])
        up_act = dot(x, wu[...])
        active = ((up_act + 1.0) * gate_act * jax.nn.sigmoid(1.702 * gate_act)).astype(BF16)
        y = dot(active, wd[...]).astype(BF16)
        for j in range(12):
            tile = y[:128, 128 * j : 128 * j + 128]
            p_mine[4 * c : 4 * c + 4, 16 * j : 16 * j + 16, :] = tile[:64].reshape(4, 16, 128)
            p_other[4 * c : 4 * c + 4, 16 * j : 16 * j + 16, :] = tile[64:].reshape(4, 16, 128)
        for g in range(3):
            tiles = jnp.concatenate([y[128:, 128 * (4 * g + j) : 128 * (4 * g + j + 1)] for j in range(4)], axis=0)
            back = dot(to_block, tiles).astype(BF16)
            p_mine[4 * c : 4 * c + 4, 192 + 16 * g : 208 + 16 * g, :] = back[:64].reshape(4, 16, 128)
            p_other[4 * c : 4 * c + 4, 192 + 16 * g : 208 + 16 * g, :] = back[64:].reshape(4, 16, 128)
        copy = pltpu.make_async_remote_copy(
            src_ref=p_other.at[pl.ds(4 * c, 4)], dst_ref=p_in.at[pl.ds(4 * c, 4)],
            send_sem=pout_sem.at[c], recv_sem=pin_sem.at[c], device_id=partner, device_id_type=MESH)
        copy.start()
        sent_pieces.append(copy)
        if c > 0:
            finish(c - 1)
    finish(3)

    for copy in sent_results:
        copy.wait_recv()
    for j in range(12):
        part = dot(combine_main, ret[:, 16 * j : 16 * j + 16, :].reshape(256, 128))
        g = j // 4
        part = part + dot(combine_tail[j % 4], ret[:, 192 + 16 * g : 208 + 16 * g, :].reshape(256, 128))
        mixed = part[:TOK] + part[TOK : 2 * TOK] + part[2 * TOK :]
        lo, hi = 128 * j, min(128 * j + 128, D)
        out_ref[:, lo:hi] = branch_ref[:, lo:hi] + mixed[:, : hi - lo]

    for copy in outgoing + forwards + sent_pieces + sent_results + kv_gather.copies + ow_gather.copies + ow_gather.given:
        copy.wait_send()


def local(
    queries, keys, values, sinks, out_weight, norm_gain, routes, gates,
    gate_codes, up_codes, down_codes, gate_scales, up_scales, down_scales,
):
    vmem = pl.BlockSpec(memory_space=pltpu.VMEM)
    hbm = pl.BlockSpec(memory_space=pl.ANY)
    dma = pltpu.SemaphoreType.DMA
    blocks = pltpu.VMEM((CHIPS, BLK, 128), BF16)
    out = pl.pallas_call(
        layer_kernel,
        out_shape=jax.ShapeDtypeStruct((TOK, D), F32),
        in_specs=[hbm] * 3 + [pl.BlockSpec(memory_space=pltpu.SMEM), hbm] + [vmem] * 3 + [hbm] * 3 + [vmem] * 3,
        out_specs=vmem,
        scratch_shapes=[
            pltpu.VMEM((TOK, QH * HD), BF16),
            pltpu.VMEM((16, TOK, 512), BF16),
            pltpu.VMEM((QH * TOK, 256), BF16),
            pltpu.VMEM((QH * TOK, 128), F32),
            pltpu.VMEM((QH * TOK, 128), F32),
            pltpu.VMEM((QH * TOK, 256), F32),
            pltpu.VMEM((64, 32, D), BF16),
            pltpu.VMEM((TOK, D), F32),
            pltpu.VMEM((TOK, DP), BF16),
            pltpu.VMEM((192, D), jnp.int32),
            pltpu.VMEM((192, D), jnp.int32),
            pltpu.VMEM((360, FF), jnp.int32),
            pltpu.VMEM((D, 192), jnp.int32),
            pltpu.VMEM((D, 192), jnp.int32),
            pltpu.VMEM((FF, 360), jnp.int32),
            pltpu.VMEM((D, DP), BF16),
            pltpu.VMEM((FF, 512), BF16),
            pltpu.VMEM((DP, FF), BF16),
            pltpu.VMEM((DP, FF), BF16),
            pltpu.VMEM((FF, DP), BF16),
            blocks, blocks, blocks, blocks, blocks, blocks, blocks, blocks,
            dma((7,)), dma((15,)), dma((15,)), dma((30,)), dma((30,)), dma((32,)), dma((32,)),
            dma((CHIPS,)), dma((CHIPS,)), dma((CHIPS,)), dma((CHIPS,)), dma((4,)), dma((4,)),
            dma((CHIPS,)), dma((CHIPS,)),
        ],
        compiler_params=pltpu.CompilerParams(collective_id=0, has_side_effects=True, vmem_limit_bytes=60 * 1024 * 1024),
        name="layer",
    )(
        queries[0], keys[0], values[0], sinks, out_weight.reshape(2, 32, D), norm_gain, routes[0].T, gates[0].T,
        gate_codes[0].T, up_codes[0].T, down_codes[0].T, jnp.swapaxes(gate_scales, 0, 1), jnp.swapaxes(up_scales, 0, 1), down_scales[0],
    )
    return out.astype(BF16)[None]


def solution(mesh):
    return jax.shard_map(
        local,
        mesh=mesh,
        in_specs=(
            P("exp", "ctx", None),
            P("exp", "ctx", None),
            P("exp", "ctx", None),
            P(),
            P("exp", None),
            P(),
            P("exp", "ctx", None),
            P("exp", "ctx", None),
            P("exp", None, None),
            P("exp", None, None),
            P("exp", None, None),
            P("exp", None, None),
            P("exp", None, None),
            P("exp", None, None),
        ),
        out_specs=P("exp", "ctx", None),
        check_vma=False,
    )
```

```python
import functools
import math

import jax
import jax.numpy as jnp
from jax import lax
from jax.experimental import pallas as pl
from jax.experimental.pallas import tpu as pltpu
from jax.sharding import PartitionSpec as P

QH = 32
KVH = 4
HD = 64
TOPK = 4
D = 1440
DP = 1536
FF = 768
TOK = 64
CHIPS = 16
BLK = 240
MESH = pl.DeviceIdType.MESH
F32 = jnp.float32
BF16 = jnp.bfloat16

OFFSETS = []
for step in range(8):
    half = (step + 1) // 2
    dz = half if step % 2 else -half
    OFFSETS += [(0, dz), (1, dz)]


def iota(shape, axis):
    return lax.broadcasted_iota(jnp.int32, shape, axis)


def dot(a, b):
    return jnp.dot(a, b, preferred_element_type=F32)


def offset_expert(i, x_hi, z):
    step = i >> 1
    half = (step + 1) >> 1
    dz = jnp.where((step & 1) == 1, half, -half)
    return ((x_hi + (i & 1)) & 1) * 8 + ((z + dz + 8) & 7)


def split3(x):
    hi = x.astype(BF16)
    rest = x - hi.astype(F32)
    mid = rest.astype(BF16)
    low = (rest - mid.astype(F32)).astype(BF16)
    return hi, mid, low


def fp4_plane(words, shift):
    code = (words >> shift) & 15
    size = code & 7
    twice = size + jnp.maximum(size - 4, 0) + 2 * jnp.maximum(size - 6, 0)
    return jnp.where(code >= 8, -twice, twice).astype(F32).astype(BF16)


def turn(source_ref, target_ref, rows, words):
    for lo in range(0, rows, 128):
        hi = min(lo + 128, rows)
        target_ref[lo:hi, :] = jnp.transpose(source_ref[:, lo:hi])


def code_planes(codes_ref, planes_ref, rows, words):
    blocks = [(b, 128 * b, min(128, words - 128 * b)) for b in range((words + 127) // 128)]

    def step(i, _):
        r = pl.multiple_of(i * 32, 32)
        for b, lo, count in blocks:
            w = codes_ref[pl.ds(r, 32), lo : lo + count]
            if count == 64:
                w = jnp.concatenate([w, w], axis=1)
                shifts = [(iota((32, 128), 1) >> 6) * 4 + 8 * k for k in range(2)]
            else:
                if count < 128:
                    w = jnp.concatenate([w, jnp.zeros((32, 128 - count), jnp.int32)], axis=1)
                shifts = [4 * k for k in range(4)]
            for k, shift in enumerate(shifts):
                at = 512 * b + 128 * k
                planes_ref[pl.ds(r, 32), at : at + 128] = fp4_plane(w, shift)
        return 0

    lax.fori_loop(0, rows // 32, step, 0)


def weight_rows(planes_ref, scales_ref, perm_ref, out_ref, rows, words, m_rows):
    groups = m_rows // 32
    blocks = [(b, min(128, words - 128 * b)) for b in range((words + 127) // 128)]
    for i in range(rows // m_rows):
        r = i * m_rows
        for b, count in blocks:
            width = 4 * count
            if count == 64:
                value = dot(planes_ref[r : r + m_rows, 512 * b : 512 * b + 256], perm_ref[512:768, :256])
            else:
                value = dot(planes_ref[r : r + m_rows, 512 * b : 512 * b + 512], perm_ref[:512, :])
            value = value[:, :width]
            scale = scales_ref[groups * i : groups * (i + 1), ..., 512 * b : 512 * b + width]
            factor = (1 << (scale - 118)).astype(F32) * (2.0**-10)
            for n in range(groups):
                piece = value[32 * n : 32 * n + 32] * (factor[n] if factor.ndim == 3 else factor[n : n + 1])
                out_ref[r + 32 * n : r + 32 * n + 32, 512 * b : 512 * b + width] = piece.astype(BF16)


class Gather:
    RELAYS = {
        ("A", 1): "+", ("A", 2): "+s", ("A", 3): "+s", ("A", 4): "s",
        ("A", -1): "-", ("A", -2): "-", ("A", -3): "s",
        ("B", 0): "+-", ("B", -1): "-",
    }

    def __init__(self, buf, index, sends, recvs, there):
        self.buf, self.index, self.sends, self.recvs = buf, index, sends, recvs
        self.there = there
        self.count = 0
        self.waits = {}
        self.copies = []

    def send(self, way, side, step):
        where = self.index(side, step)
        if way == "+":
            name = (side, step + 1)
        elif way == "-":
            name = (side, step - 1)
        else:
            name = ("B", step)
        copy = pltpu.make_async_remote_copy(
            src_ref=self.buf.at[where], dst_ref=self.buf.at[where], send_sem=self.sends.at[self.count],
            recv_sem=self.recvs.at[self.count], device_id=self.there[way], device_id_type=MESH)
        copy.start()
        self.count += 1
        self.copies.append(copy)
        self.waits[name] = copy

    def begin(self):
        for way in "+-s":
            self.send(way, "A", 0)

    def take(self, side, step):
        self.waits[side, step].wait_recv()
        for way in self.RELAYS.get((side, step), ""):
            self.send(way, side, step)


class WeightGather:
    def __init__(self, buf, unit, turn, there, partner, sems):
        self.buf, self.unit, self.sign, self.there, self.partner = buf, unit, turn, there, partner
        self.sends, self.recvs, self.give_sends, self.give_recvs = sems
        self.copies, self.given, self.by_name, self.given_by = [], [], {}, {}

    def send(self, name, way, side, step, half):
        where = self.unit(side, step, half)
        n = len(self.copies)
        copy = pltpu.make_async_remote_copy(
            src_ref=self.buf.at[where], dst_ref=self.buf.at[where], send_sem=self.sends.at[n],
            recv_sem=self.recvs.at[n], device_id=self.there[way], device_id_type=MESH)
        copy.start()
        self.copies.append(copy)
        self.by_name[name + (half,)] = copy

    def give(self, name, side, step, half):
        where = self.unit(side, step, half)
        n = len(self.given)
        copy = pltpu.make_async_remote_copy(
            src_ref=self.buf.at[where], dst_ref=self.buf.at[where], send_sem=self.give_sends.at[n],
            recv_sem=self.give_recvs.at[n], device_id=self.partner, device_id_type=MESH)
        copy.start()
        self.given.append(copy)
        self.given_by[name] = self.given_by.get(name, []) + [copy]

    def begin(self):
        for half in range(2):
            self.send(("A", 1), "+", "A", 0, half)
            self.send(("A", -1), "-", "A", 0, half)
            self.send(("B", 0), "cross", "A", 0, half)
        for half in range(2):
            self.give(("A", 0), "A", 0, half)

    def ring(self, k, half):
        ways = [1, -1] if k < 4 else [1 if half == 0 else -1]
        for way in ways:
            self.by_name["A", way * k, half].wait_recv()
        for way in ways:
            if k < 3 or (k == 3 and (half == 0) == (way == 1)):
                self.send(("A", way * (k + 1)), "+" if way == 1 else "-", "A", way * k, half)
        if k < 4:
            self.send(("B", "near", k), "cross", "A", -self.sign * k, half)
        else:
            self.send(("B", 4), "cross", "A", 4, half)
        for way in ways:
            self.give(("A", way * k if k < 4 else 4), "A", way * k, half)

    def near(self, k, half):
        self.by_name["B", "near", k, half].wait_recv()
        self.send(("B", "far", k), "pair", "B", self.sign * k, half)
        self.give(("near", k), "B", self.sign * k, half)

    def far(self, k, half):
        self.by_name["B", "far", k, half].wait_recv()
        self.give(("far", k), "B", -self.sign * k, half)

    def other(self, k, half):
        self.by_name["B", k, half].wait_recv()
        self.give(("B", k), "B", k, half)


def layer_kernel(
    queries_hbm, keys_hbm, values_hbm, sinks_ref, ow_hbm, gain_ref, routes_t_ref, gates_t_ref,
    gc_hbm, uc_hbm, dc_hbm, gs, us, ds,
    out_ref,
    q_in, kv, qz, tops, totals, heads, attended, wbuf, branch_ref, normed_ref,
    gct, uct, dct, gc, uc, dc, planes, perm, wg, wu, wd,
    send, mine, other, p_mine, p_other, p_in, result, ret,
    in_sem, kv_send, kv_recv, ow_send, ow_recv, give_send, give_recv,
    send_sem, mine_sem, fwd_sem, other_sem, pout_sem, pin_sem, res_sem, ret_sem,
):
    me = lax.axis_index("exp")
    ctx = lax.axis_index("ctx")
    core = me & 1
    z = (me >> 1) & 7
    x_hi = me >> 4
    y = ctx >> 1
    x_lo = ctx & 1

    def peer(i):
        dx, dz = OFFSETS[i]
        return {"exp": (((x_hi + dx) & 1) * 8 + ((z + dz + 8) & 7)) * 2 + core, "ctx": ctx ^ dx}

    def source(i):
        dx, dz = OFFSETS[i]
        return {"exp": (((x_hi + dx) & 1) * 8 + ((z - dz + 8) & 7)) * 2 + core, "ctx": ctx ^ dx}

    partner = {"exp": me ^ 1}
    kv_there = {
        "+": {"ctx": ((y + 1) & 7) * 2 + x_lo}, "-": {"ctx": ((y + 7) & 7) * 2 + x_lo}, "s": {"ctx": ctx ^ 1},
    }
    ow_there = {
        "+": {"exp": (x_hi * 8 + ((z + 1) & 7)) * 2 + core}, "-": {"exp": (x_hi * 8 + ((z + 7) & 7)) * 2 + core},
        "cross": {"ctx": ctx ^ 1, "exp": me ^ 16}, "pair": {"ctx": ctx ^ 1},
    }

    def kv_index(side, step):
        return ((y - step + 8) & 7) * 2 + (x_lo if side == "A" else 1 - x_lo)

    def ow_unit(side, step, half):
        return (((x_hi if side == "A" else 1 - x_hi) * 8 + ((z - step + 8) & 7)) * 2 + core) * 2 + half

    kv_gather = Gather(kv, kv_index, kv_send, kv_recv, kv_there)
    ow_gather = WeightGather(
        wbuf, ow_unit, 1 - 2 * x_lo, ow_there, partner, (ow_send, ow_recv, give_send, give_recv))

    barrier = pltpu.get_barrier_semaphore()
    greeted = [peer(i) for i in range(1, CHIPS)] + [partner, kv_there["+"], kv_there["-"], kv_there["s"]]
    for device in greeted:
        pl.semaphore_signal(barrier, inc=1, device_id=device, device_id_type=MESH)

    loads = []
    for n, (src, dst) in enumerate((
        (keys_hbm, kv.at[ctx, :, 0:256]), (values_hbm, kv.at[ctx, :, 256:512]), (ow_hbm, wbuf.at[pl.ds(2 * me, 2)]),
        (gc_hbm, gct), (uc_hbm, uct), (dc_hbm, dct), (queries_hbm, q_in),
    )):
        copy = pltpu.make_async_copy(src, dst, in_sem.at[n])
        copy.start()
        loads.append(copy)
    loads[0].wait()
    loads[1].wait()
    loads[2].wait()
    pl.semaphore_wait(barrier, len(greeted))
    kv_gather.begin()
    ow_gather.begin()

    loads[6].wait()
    left = iota((TOK, 128), 1) < 64
    for h in range(QH):
        g = h // 8
        tile = q_in[:, 128 * (h // 2) : 128 * (h // 2) + 128].astype(F32) * (1.0 / math.sqrt(HD))
        if h % 2 != g % 2:
            tile = pltpu.roll(tile, 64, 1)
        tile = jnp.where(left if g % 2 == 0 else ~left, tile, 0.0).astype(BF16)
        lo = 128 * (g // 2)
        qz[64 * h : 64 * h + 64, lo : lo + 128] = tile
        qz[64 * h : 64 * h + 64, 128 - lo : 256 - lo] = jnp.zeros((TOK, 128), BF16)
        tops[64 * h : 64 * h + 64, :] = jnp.broadcast_to(sinks_ref[h], (TOK, 128))
    normed_ref[:, D:] = jnp.zeros((TOK, DP - D), BF16)

    def attend(names, part, first=False):
        where = [kv_index(*name) for name in names]
        lane = iota((TOK, 256), 1)
        owner = jnp.where(lane < 128, jnp.where(lane < 64, where[0], where[1]), jnp.where(lane < 192, where[2], where[3]))
        bias = jnp.where(owner * TOK + (lane & 63) <= ctx * TOK + iota((TOK, 256), 0), 0.0, -1e30)

        def rows(i, _):
            r = pl.multiple_of(i * 512, 512)
            key_block = jnp.concatenate([kv[w, :, 0:256] for w in where], axis=0)
            value_block = jnp.concatenate([kv[w, :, 256:512] for w in where], axis=0)
            scores = lax.dot_general(
                qz[pl.ds(r, 512), :], key_block, (((1,), (1,)), ((), ())), preferred_element_type=F32)
            scores = (scores.reshape(8, TOK, 256) + bias[None]).reshape(512, 256)
            old = tops[pl.ds(r, 512), :1]
            top = jnp.maximum(jnp.max(scores, axis=1, keepdims=True), old)
            prob = jnp.exp(scores - top)
            shrink = jnp.exp(old - top)
            added = jnp.sum(prob, axis=1, keepdims=True)
            value = dot(prob.astype(BF16), value_block)
            tops[pl.ds(r, 512), :] = jnp.broadcast_to(top, (512, 128))
            if first:
                totals[pl.ds(r, 512), :] = jnp.broadcast_to(shrink + added, (512, 128))
                heads[pl.ds(r, 512), :] = value
            else:
                totals[pl.ds(r, 512), :] = totals[pl.ds(r, 512), :] * shrink + added
                heads[pl.ds(r, 512), :] = heads[pl.ds(r, 512), :] * shrink + value
            return 0

        lax.fori_loop(2 * part, 2 * part + 2, rows, 0)

    def take(*names):
        for name in names:
            kv_gather.take(*name)

    chunks = [
        (("A", 0), ("A", 1), ("A", -1), ("B", 0)), (("A", 2), ("A", -2), ("B", 1), ("B", -1)),
        (("A", 3), ("A", -3), ("B", 2), ("B", -2)), (("A", 4), ("B", 3), ("B", -3), ("B", 4)),
    ]
    take(*chunks[0][1:])
    ow_gather.ring(1, 0)
    attend(chunks[0], 0, True)
    ow_gather.ring(1, 1)
    take(("A", 2), ("A", -2))
    attend(chunks[0], 1, True)
    ow_gather.other(0, 0)
    ow_gather.other(0, 1)
    take(("B", 1), ("B", -1))
    ow_gather.ring(2, 0)
    take(("A", 3), ("A", -3))
    ow_gather.near(1, 0)
    ow_gather.near(1, 1)
    attend(chunks[1], 0)
    ow_gather.ring(2, 1)
    take(("B", 2), ("B", -2))
    attend(chunks[1], 1)
    take(("A", 4),)
    ow_gather.ring(3, 0)
    ow_gather.near(2, 0)
    attend(chunks[2], 0)
    ow_gather.near(2, 1)
    attend(chunks[2], 1)
    ow_gather.far(1, 0)
    ow_gather.far(1, 1)
    ow_gather.ring(3, 1)
    take(("B", 3), ("B", -3), ("B", 4))
    ow_gather.near(3, 0)
    attend(chunks[3], 0)
    ow_gather.ring(4, 0)
    ow_gather.ring(4, 1)
    attend(chunks[3], 1)
    ow_gather.near(3, 1)
    for half in range(2):
        ow_gather.far(2, half)

    for m in range(QH // 2):
        g = m // 4
        pair = []
        for h in (2 * m, 2 * m + 1):
            tile = heads[64 * h : 64 * h + 64, 128 * (g // 2) : 128 * (g // 2) + 128]
            tile = tile / totals[64 * h : 64 * h + 64, :]
            pair.append(pltpu.roll(tile, 64, 1) if h % 2 != g % 2 else tile)
        attended[m] = jnp.where(left, pair[0], pair[1]).astype(BF16)

    def project(blocks):
        chips = [(x_hi if side == "A" else 1 - x_hi) * 8 + ((z - step + 8) & 7) for side, step in blocks]
        return dot(
            jnp.concatenate([attended[m] for m in chips], axis=1),
            jnp.concatenate([wbuf[pl.ds(4 * m, 4)].reshape(128, D) for m in chips], axis=0))

    for name in (("A", 0), ("A", 1), ("A", -1), ("A", 2), ("A", -2), ("B", 0), ("near", 1), ("far", 1)):
        for copy in ow_gather.given_by[name]:
            copy.wait_recv()
    branch = project([("A", 0), ("A", 1), ("A", -1), ("A", 2), ("A", -2), ("B", 0), ("B", 1), ("B", -1)])
    for half in range(2):
        ow_gather.far(3, half)
        ow_gather.other(4, half)
    for name in (("A", 3), ("A", -3), ("A", 4), ("near", 2), ("far", 2), ("near", 3), ("far", 3), ("B", 4)):
        for copy in ow_gather.given_by[name]:
            copy.wait_recv()
    branch = branch + project(
        [("A", 3), ("A", -3), ("A", 4), ("B", 2), ("B", -2), ("B", 3), ("B", -3), ("B", 4)])
    branch_ref[...] = branch
    mean_sq = jnp.sum(branch * branch, axis=1, keepdims=True) * (1.0 / D)
    normed_ref[:, :D] = (branch * lax.rsqrt(mean_sq + 1e-05) * gain_ref[...].reshape(1, D)).astype(BF16)

    routes_t = routes_t_ref[...]
    expert = offset_expert(iota((CHIPS, TOK), 0), x_hi, z)
    hit = jnp.zeros((CHIPS, TOK), F32)
    for k in range(TOPK):
        hit = hit + (routes_t[k : k + 1, :] == expert).astype(F32)
    before = (iota((TOK, 256), 0) < (iota((TOK, 256), 1) & 63)).astype(BF16)
    same = (iota((TOK, 256), 0) == (iota((TOK, 256), 1) & 63)).astype(BF16)
    hit16 = hit.astype(BF16)
    slot4 = dot(hit16, before)
    hit4 = dot(hit16, same)
    slot4 = jnp.where(hit4 > 0.5, slot4, -1000.0)
    slot_i = slot4.astype(jnp.int32)
    slot_main = slot_i[:, :TOK]
    pick = (jnp.broadcast_to(slot_main[:, None, :], (CHIPS, 16, TOK)) == iota((CHIPS, 16, TOK), 1)).astype(F32)
    pick = pick.astype(BF16).reshape(CHIPS * 16, TOK)
    rows = dot(pick, normed_ref[...]).astype(BF16)
    for j in range(12):
        send[:, 16 * j : 16 * j + 16, :] = rows[:, 128 * j : 128 * j + 128].reshape(CHIPS, 16, 128)
    tail_key = jnp.where(slot_i >= 16, slot_i - 16 + 4 * (iota((CHIPS, 256), 1) >> 6), -1)
    tail = (jnp.broadcast_to(tail_key[:, None, :], (CHIPS, 16, 256)) == iota((CHIPS, 16, 256), 1)).astype(F32)
    tail = tail.astype(BF16).reshape(CHIPS * 16, 256)
    for g in range(3):
        stacked = jnp.concatenate([normed_ref[:, 128 * (4 * g + j) : 128 * (4 * g + j + 1)] for j in range(4)], axis=0)
        send[:, 192 + 16 * g : 208 + 16 * g, :] = dot(tail, stacked).astype(BF16).reshape(CHIPS, 16, 128)

    outgoing = {}
    for i in reversed(range(1, CHIPS)):
        copy = pltpu.make_async_remote_copy(
            src_ref=send.at[i], dst_ref=mine.at[i], send_sem=send_sem.at[i], recv_sem=mine_sem.at[i],
            device_id=peer(i), device_id_type=MESH)
        copy.start()
        outgoing[i] = copy

    def forward(i):
        copy = pltpu.make_async_remote_copy(
            src_ref=send.at[0] if i == 0 else mine.at[i], dst_ref=other.at[i],
            send_sem=fwd_sem.at[i], recv_sem=other_sem.at[i],
            device_id=partner, device_id_type=MESH)
        copy.start()
        return copy

    forwards = {0: forward(0)}

    padded = jnp.concatenate(
        [routes_t.astype(F32), gates_t_ref[...]], axis=0)
    padded = jnp.transpose(jnp.concatenate([padded, jnp.zeros((8, 64), F32)], axis=1))[:TOK, :]
    routes = padded[:, :TOPK].astype(jnp.int32)
    gates = padded[:, TOPK:]
    expert_of = offset_expert(iota((TOK, CHIPS), 1), x_hi, z)
    hits = jnp.zeros((TOK, CHIPS), F32)
    for k in range(TOPK):
        hits = hits + (routes[:, k : k + 1] == expert_of).astype(F32)
    earlier = (iota((TOK, TOK), 1) < iota((TOK, TOK), 0)).astype(BF16)
    slots = jnp.where(hits > 0.5, dot(earlier, hits.astype(BF16)), 100.0)
    spread = (iota((CHIPS, 256), 0) == (iota((CHIPS, 256), 1) >> 4)).astype(BF16)
    slots = dot(slots.astype(BF16), spread).astype(jnp.int32)
    column_expert = offset_expert(iota((TOK, 256), 1) >> 4, x_hi, z)
    weight = jnp.zeros((TOK, 256), F32)
    for k in range(TOPK):
        weight = weight + jnp.where(routes[:, k : k + 1] == column_expert, gates[:, k : k + 1], 0.0)
    place = iota((TOK, 256), 1) & 15
    combine_main = jnp.concatenate(split3(jnp.where(slots == place, weight, 0.0)), axis=0)
    combine_tail = [
        jnp.concatenate(split3(jnp.where((slots - 16 == (place & 3)) & ((place >> 2) == j), weight, 0.0)), axis=0)
        for j in range(4)
    ]

    wide = iota((512, 512), 0)
    perm[:512, :] = (iota((512, 512), 1) == 4 * (wide & 127) + (wide >> 7)).astype(F32).astype(BF16)
    narrow = iota((256, 512), 0)
    perm[512:768, :] = (iota((256, 512), 1) == 4 * (narrow & 63) + (narrow >> 6)).astype(F32).astype(BF16)
    wg[D:, :] = jnp.zeros((DP - D, FF), BF16)
    wu[D:, :] = jnp.zeros((DP - D, FF), BF16)
    wd[:, D:] = jnp.zeros((FF, DP - D), BF16)
    loads[3].wait()
    turn(gct, gc, D, 192)
    code_planes(gc, planes, D, 192)
    weight_rows(planes, gs, perm, wg, D, 192, 288)
    loads[4].wait()
    turn(uct, uc, D, 192)
    code_planes(uc, planes, D, 192)
    weight_rows(planes, us, perm, wu, D, 192, 288)
    loads[5].wait()
    turn(dct, dc, FF, 360)
    code_planes(dc, planes, FF, 360)
    weight_rows(planes, ds, perm, wd, FF, 360, 256)

    a, b = iota((128, 128), 0), iota((128, 128), 1)
    to_rows = (b == ((a >> 2) & 7) * 16 + (a >> 5) * 4 + (a & 3)).astype(F32).astype(BF16)
    to_block = (a == ((b >> 2) & 7) * 16 + (b >> 5) * 4 + (b & 3)).astype(F32).astype(BF16)

    sent_pieces = {}
    sent_results = []
    done = []

    def finish(c):
        sent_pieces[c].wait_recv()
        for i in range(4 * c, 4 * c + 4):
            total = (p_mine[i].astype(F32) + p_in[i].astype(F32)).astype(BF16)
            if i == 0:
                ret[0] = total
            else:
                result[i] = total
        for i in reversed(range(max(1, 4 * c), 4 * c + 4)):
            copy = pltpu.make_async_remote_copy(
                src_ref=result.at[i], dst_ref=ret.at[i], send_sem=res_sem.at[i], recv_sem=ret_sem.at[i],
                device_id=source(i), device_id_type=MESH)
            copy.start()
            sent_results.append(copy)

    for c in (3, 2, 1, 0):
        for i in reversed(range(max(1, 4 * c), 4 * c + 4)):
            outgoing[i].wait_recv()
            forwards[i] = forward(i)
        for i in range(4 * c, 4 * c + 4):
            forwards[i].wait_recv()
        if c == 0:
            mine[0] = send[0]

        def both(lo, hi):
            return jnp.concatenate(
                [mine[4 * c : 4 * c + 4, lo:hi, :].reshape(64, 128), other[4 * c : 4 * c + 4, lo:hi, :].reshape(64, 128)],
                axis=0)

        main = jnp.concatenate([both(16 * j, 16 * j + 16) for j in range(12)], axis=1)
        tails = []
        for g in range(3):
            moved = dot(to_rows, both(192 + 16 * g, 208 + 16 * g)).astype(BF16)
            tails += [moved[32 * j : 32 * j + 32, :] for j in range(4)]
        x = jnp.concatenate([main, jnp.concatenate(tails, axis=1)], axis=0)
        gate_act = dot(x, wg[...])
        up_act = dot(x, wu[...])
        active = ((up_act + 1.0) * gate_act * jax.nn.sigmoid(1.702 * gate_act)).astype(BF16)
        y = dot(active, wd[...]).astype(BF16)
        for j in range(12):
            tile = y[:128, 128 * j : 128 * j + 128]
            p_mine[4 * c : 4 * c + 4, 16 * j : 16 * j + 16, :] = tile[:64].reshape(4, 16, 128)
            p_other[4 * c : 4 * c + 4, 16 * j : 16 * j + 16, :] = tile[64:].reshape(4, 16, 128)
        for g in range(3):
            tiles = jnp.concatenate([y[128:, 128 * (4 * g + j) : 128 * (4 * g + j + 1)] for j in range(4)], axis=0)
            back = dot(to_block, tiles).astype(BF16)
            p_mine[4 * c : 4 * c + 4, 192 + 16 * g : 208 + 16 * g, :] = back[:64].reshape(4, 16, 128)
            p_other[4 * c : 4 * c + 4, 192 + 16 * g : 208 + 16 * g, :] = back[64:].reshape(4, 16, 128)
        copy = pltpu.make_async_remote_copy(
            src_ref=p_other.at[pl.ds(4 * c, 4)], dst_ref=p_in.at[pl.ds(4 * c, 4)],
            send_sem=pout_sem.at[c], recv_sem=pin_sem.at[c], device_id=partner, device_id_type=MESH)
        copy.start()
        sent_pieces[c] = copy
        if done:
            finish(done[-1])
        done.append(c)
    finish(0)

    for copy in sent_results:
        copy.wait_recv()
    for j in range(12):
        part = dot(combine_main, ret[:, 16 * j : 16 * j + 16, :].reshape(256, 128))
        g = j // 4
        part = part + dot(combine_tail[j % 4], ret[:, 192 + 16 * g : 208 + 16 * g, :].reshape(256, 128))
        mixed = part[:TOK] + part[TOK : 2 * TOK] + part[2 * TOK :]
        lo, hi = 128 * j, min(128 * j + 128, D)
        out_ref[:, lo:hi] = branch_ref[:, lo:hi] + mixed[:, : hi - lo]

    for copy in list(outgoing.values()) + list(forwards.values()) + list(sent_pieces.values()) + sent_results + kv_gather.copies + ow_gather.copies + ow_gather.given:
        copy.wait_send()


def local(
    queries, keys, values, sinks, out_weight, norm_gain, routes, gates,
    gate_codes, up_codes, down_codes, gate_scales, up_scales, down_scales,
):
    vmem = pl.BlockSpec(memory_space=pltpu.VMEM)
    hbm = pl.BlockSpec(memory_space=pl.ANY)
    dma = pltpu.SemaphoreType.DMA
    blocks = pltpu.VMEM((CHIPS, BLK, 128), BF16)
    out = pl.pallas_call(
        layer_kernel,
        out_shape=jax.ShapeDtypeStruct((TOK, D), F32),
        in_specs=[hbm] * 3 + [pl.BlockSpec(memory_space=pltpu.SMEM), hbm] + [vmem] * 3 + [hbm] * 3 + [vmem] * 3,
        out_specs=vmem,
        scratch_shapes=[
            pltpu.VMEM((TOK, QH * HD), BF16),
            pltpu.VMEM((16, TOK, 512), BF16),
            pltpu.VMEM((QH * TOK, 256), BF16),
            pltpu.VMEM((QH * TOK, 128), F32),
            pltpu.VMEM((QH * TOK, 128), F32),
            pltpu.VMEM((QH * TOK, 256), F32),
            pltpu.VMEM((QH // 2, TOK, 128), BF16),
            pltpu.VMEM((64, 32, D), BF16),
            pltpu.VMEM((TOK, D), F32),
            pltpu.VMEM((TOK, DP), BF16),
            pltpu.VMEM((192, D), jnp.int32),
            pltpu.VMEM((192, D), jnp.int32),
            pltpu.VMEM((360, FF), jnp.int32),
            pltpu.VMEM((D, 192), jnp.int32),
            pltpu.VMEM((D, 192), jnp.int32),
            pltpu.VMEM((FF, 360), jnp.int32),
            pltpu.VMEM((D, DP), BF16),
            pltpu.VMEM((FF, 512), BF16),
            pltpu.VMEM((DP, FF), BF16),
            pltpu.VMEM((DP, FF), BF16),
            pltpu.VMEM((FF, DP), BF16),
            blocks, blocks, blocks, blocks, blocks, blocks, blocks, blocks,
            dma((7,)), dma((15,)), dma((15,)), dma((30,)), dma((30,)), dma((32,)), dma((32,)),
            dma((CHIPS,)), dma((CHIPS,)), dma((CHIPS,)), dma((CHIPS,)), dma((4,)), dma((4,)),
            dma((CHIPS,)), dma((CHIPS,)),
        ],
        compiler_params=pltpu.CompilerParams(collective_id=0, has_side_effects=True, vmem_limit_bytes=60 * 1024 * 1024),
        name="layer",
    )(
        queries[0], keys[0], values[0], sinks, out_weight.reshape(2, 32, D), norm_gain, routes[0].T, gates[0].T,
        gate_codes[0].T, up_codes[0].T, down_codes[0].T, jnp.swapaxes(gate_scales, 0, 1), jnp.swapaxes(up_scales, 0, 1), down_scales[0],
    )
    return out.astype(BF16)[None]


def solution(mesh):
    return jax.shard_map(
        local,
        mesh=mesh,
        in_specs=(
            P("exp", "ctx", None),
            P("exp", "ctx", None),
            P("exp", "ctx", None),
            P(),
            P("exp", None),
            P(),
            P("exp", "ctx", None),
            P("exp", "ctx", None),
            P("exp", None, None),
            P("exp", None, None),
            P("exp", None, None),
            P("exp", None, None),
            P("exp", None, None),
            P("exp", None, None),
        ),
        out_specs=P("exp", "ctx", None),
        check_vma=False,
    )
```

```python
import functools
import math

import jax
import jax.numpy as jnp
from jax import lax
from jax.experimental import pallas as pl
from jax.experimental.pallas import tpu as pltpu
from jax.sharding import PartitionSpec as P

QH = 32
KVH = 4
HD = 64
TOPK = 4
D = 1440
DP = 1536
FF = 768
TOK = 64
CHIPS = 16
BLK = 240
GROUP = 4
MESH = pl.DeviceIdType.MESH
F32 = jnp.float32
BF16 = jnp.bfloat16

OFFSETS = []
for step in range(8):
    half = (step + 1) // 2
    dz = half if step % 2 else -half
    OFFSETS += [(0, dz), (1, dz)]


def iota(shape, axis):
    return lax.broadcasted_iota(jnp.int32, shape, axis)


def dot(a, b):
    return jnp.dot(a, b, preferred_element_type=F32)


def offset_expert(i, x_hi, z):
    step = i >> 1
    half = (step + 1) >> 1
    dz = jnp.where((step & 1) == 1, half, -half)
    return ((x_hi + (i & 1)) & 1) * 8 + ((z + dz + 8) & 7)


def split3(x):
    hi = x.astype(BF16)
    rest = x - hi.astype(F32)
    mid = rest.astype(BF16)
    low = (rest - mid.astype(F32)).astype(BF16)
    return hi, mid, low


def fp4_plane(words, shift):
    code = (words >> shift) & 15
    size = code & 7
    twice = size + jnp.maximum(size - 4, 0) + 2 * jnp.maximum(size - 6, 0)
    return jnp.where(code >= 8, -twice, twice).astype(F32).astype(BF16)


def turn(source_ref, target_ref, rows, words):
    for lo in range(0, rows, 128):
        hi = min(lo + 128, rows)
        target_ref[lo:hi, :] = jnp.transpose(source_ref[:, lo:hi])


def code_planes(codes_ref, planes_ref, rows, words):
    blocks = [(b, 128 * b, min(128, words - 128 * b)) for b in range((words + 127) // 128)]

    def step(i, _):
        r = pl.multiple_of(i * 32, 32)
        for b, lo, count in blocks:
            w = codes_ref[pl.ds(r, 32), lo : lo + count]
            if count == 64:
                w = jnp.concatenate([w, w], axis=1)
                shifts = [(iota((32, 128), 1) >> 6) * 4 + 8 * k for k in range(2)]
            else:
                if count < 128:
                    w = jnp.concatenate([w, jnp.zeros((32, 128 - count), jnp.int32)], axis=1)
                shifts = [4 * k for k in range(4)]
            for k, shift in enumerate(shifts):
                at = 512 * b + 128 * k
                planes_ref[pl.ds(r, 32), at : at + 128] = fp4_plane(w, shift)
        return 0

    lax.fori_loop(0, rows // 32, step, 0)


def weight_rows(planes_ref, scales_ref, perm_ref, out_ref, rows, words, m_rows):
    groups = m_rows // 32
    blocks = [(b, min(128, words - 128 * b)) for b in range((words + 127) // 128)]
    for i in range(rows // m_rows):
        r = i * m_rows
        for b, count in blocks:
            width = 4 * count
            if count == 64:
                value = dot(planes_ref[r : r + m_rows, 512 * b : 512 * b + 256], perm_ref[512:768, :256])
            else:
                value = dot(planes_ref[r : r + m_rows, 512 * b : 512 * b + 512], perm_ref[:512, :])
            value = value[:, :width]
            scale = scales_ref[groups * i : groups * (i + 1), ..., 512 * b : 512 * b + width]
            factor = (1 << (scale - 118)).astype(F32) * (2.0**-10)
            for n in range(groups):
                piece = value[32 * n : 32 * n + 32] * (factor[n] if factor.ndim == 3 else factor[n : n + 1])
                out_ref[r + 32 * n : r + 32 * n + 32, 512 * b : 512 * b + width] = piece.astype(BF16)


class Gather:
    RELAYS = {
        ("A", 1): "+", ("A", 2): "+s", ("A", 3): "+s", ("A", 4): "s",
        ("A", -1): "-", ("A", -2): "-", ("A", -3): "s",
        ("B", 0): "+-", ("B", -1): "-",
    }

    def __init__(self, buf, index, sends, recvs, there):
        self.buf, self.index, self.sends, self.recvs = buf, index, sends, recvs
        self.there = there
        self.count = 0
        self.waits = {}
        self.copies = []

    def send(self, way, side, step):
        where = self.index(side, step)
        if way == "+":
            name = (side, step + 1)
        elif way == "-":
            name = (side, step - 1)
        else:
            name = ("B", step)
        copy = pltpu.make_async_remote_copy(
            src_ref=self.buf.at[where], dst_ref=self.buf.at[where], send_sem=self.sends.at[self.count],
            recv_sem=self.recvs.at[self.count], device_id=self.there[way], device_id_type=MESH)
        copy.start()
        self.count += 1
        self.copies.append(copy)
        self.waits[name] = copy

    def begin(self):
        for way in "+-s":
            self.send(way, "A", 0)

    def take(self, side, step):
        self.waits[side, step].wait_recv()
        for way in self.RELAYS.get((side, step), ""):
            self.send(way, side, step)


class WeightGather:
    def __init__(self, buf, unit, turn, there, partner, sems):
        self.buf, self.unit, self.sign, self.there, self.partner = buf, unit, turn, there, partner
        self.sends, self.recvs, self.give_sends, self.give_recvs = sems
        self.copies, self.given, self.by_name, self.given_by = [], [], {}, {}

    def send(self, name, way, side, step, half):
        where = self.unit(side, step, half)
        n = len(self.copies)
        copy = pltpu.make_async_remote_copy(
            src_ref=self.buf.at[where], dst_ref=self.buf.at[where], send_sem=self.sends.at[n],
            recv_sem=self.recvs.at[n], device_id=self.there[way], device_id_type=MESH)
        copy.start()
        self.copies.append(copy)
        self.by_name[name + (half,)] = copy

    def give(self, name, side, step, half):
        where = self.unit(side, step, half)
        n = len(self.given)
        copy = pltpu.make_async_remote_copy(
            src_ref=self.buf.at[where], dst_ref=self.buf.at[where], send_sem=self.give_sends.at[n],
            recv_sem=self.give_recvs.at[n], device_id=self.partner, device_id_type=MESH)
        copy.start()
        self.given.append(copy)
        self.given_by[name] = self.given_by.get(name, []) + [copy]

    def begin(self):
        for half in range(2):
            self.send(("A", 1), "+", "A", 0, half)
            self.send(("A", -1), "-", "A", 0, half)
            self.send(("B", 0), "cross", "A", 0, half)
        for half in range(2):
            self.give(("A", 0), "A", 0, half)

    def ring(self, k, half):
        ways = [1, -1] if k < 4 else [1 if half == 0 else -1]
        for way in ways:
            self.by_name["A", way * k, half].wait_recv()
        for way in ways:
            if k < 3 or (k == 3 and (half == 0) == (way == 1)):
                self.send(("A", way * (k + 1)), "+" if way == 1 else "-", "A", way * k, half)
        if k < 4:
            self.send(("B", "near", k), "cross", "A", -self.sign * k, half)
        else:
            self.send(("B", 4), "cross", "A", 4, half)
        for way in ways:
            self.give(("A", way * k if k < 4 else 4), "A", way * k, half)

    def near(self, k, half):
        self.by_name["B", "near", k, half].wait_recv()
        self.send(("B", "far", k), "pair", "B", self.sign * k, half)
        self.give(("near", k), "B", self.sign * k, half)

    def far(self, k, half):
        self.by_name["B", "far", k, half].wait_recv()
        self.give(("far", k), "B", -self.sign * k, half)

    def other(self, k, half):
        self.by_name["B", k, half].wait_recv()
        self.give(("B", k), "B", k, half)


def layer_kernel(
    queries_hbm, keys_hbm, values_hbm, sinks_ref, ow_hbm, gain_ref, routes_t_ref, gates_t_ref,
    gc_hbm, uc_hbm, dc_hbm, gs, us, ds,
    out_ref,
    q_in, kv, qz, tops, totals, heads, attended, wbuf, branch_ref, normed_ref,
    gct, uct, dct, gc, uc, dc, planes, perm, wg, wu, wd,
    send, mine, other, p_mine, p_other, p_in, result, ret,
    in_sem, kv_send, kv_recv, ow_send, ow_recv, give_send, give_recv,
    send_sem, mine_sem, fwd_sem, other_sem, pout_sem, pin_sem, res_sem, ret_sem,
):
    me = lax.axis_index("exp")
    ctx = lax.axis_index("ctx")
    core = me & 1
    z = (me >> 1) & 7
    x_hi = me >> 4
    y = ctx >> 1
    x_lo = ctx & 1

    def peer(i):
        dx, dz = OFFSETS[i]
        return {"exp": (((x_hi + dx) & 1) * 8 + ((z + dz + 8) & 7)) * 2 + core, "ctx": ctx ^ dx}

    def source(i):
        dx, dz = OFFSETS[i]
        return {"exp": (((x_hi + dx) & 1) * 8 + ((z - dz + 8) & 7)) * 2 + core, "ctx": ctx ^ dx}

    partner = {"exp": me ^ 1}
    kv_there = {
        "+": {"ctx": ((y + 1) & 7) * 2 + x_lo}, "-": {"ctx": ((y + 7) & 7) * 2 + x_lo}, "s": {"ctx": ctx ^ 1},
    }
    ow_there = {
        "+": {"exp": (x_hi * 8 + ((z + 1) & 7)) * 2 + core}, "-": {"exp": (x_hi * 8 + ((z + 7) & 7)) * 2 + core},
        "cross": {"ctx": ctx ^ 1, "exp": me ^ 16}, "pair": {"ctx": ctx ^ 1},
    }

    def kv_index(side, step):
        return ((y - step + 8) & 7) * 2 + (x_lo if side == "A" else 1 - x_lo)

    def ow_unit(side, step, half):
        return (((x_hi if side == "A" else 1 - x_hi) * 8 + ((z - step + 8) & 7)) * 2 + core) * 2 + half

    kv_gather = Gather(kv, kv_index, kv_send, kv_recv, kv_there)
    ow_gather = WeightGather(
        wbuf, ow_unit, 1 - 2 * x_lo, ow_there, partner, (ow_send, ow_recv, give_send, give_recv))

    barrier = pltpu.get_barrier_semaphore()
    greeted = [peer(i) for i in range(1, CHIPS)] + [partner, kv_there["+"], kv_there["-"], kv_there["s"]]
    for device in greeted:
        pl.semaphore_signal(barrier, inc=1, device_id=device, device_id_type=MESH)

    loads = []
    for n, (src, dst) in enumerate((
        (keys_hbm, kv.at[ctx, :, 0:256]), (values_hbm, kv.at[ctx, :, 256:512]), (ow_hbm, wbuf.at[pl.ds(2 * me, 2)]),
        (gc_hbm, gct), (uc_hbm, uct), (dc_hbm, dct), (queries_hbm, q_in),
    )):
        copy = pltpu.make_async_copy(src, dst, in_sem.at[n])
        copy.start()
        loads.append(copy)
    loads[0].wait()
    loads[1].wait()
    loads[2].wait()
    pl.semaphore_wait(barrier, len(greeted))
    kv_gather.begin()
    ow_gather.begin()

    loads[6].wait()
    left = iota((TOK, 128), 1) < 64
    for h in range(QH):
        g = h // 8
        tile = q_in[:, 128 * (h // 2) : 128 * (h // 2) + 128].astype(F32) * (1.0 / math.sqrt(HD))
        if h % 2 != g % 2:
            tile = pltpu.roll(tile, 64, 1)
        tile = jnp.where(left if g % 2 == 0 else ~left, tile, 0.0).astype(BF16)
        lo = 128 * (g // 2)
        qz[64 * h : 64 * h + 64, lo : lo + 128] = tile
        qz[64 * h : 64 * h + 64, 128 - lo : 256 - lo] = jnp.zeros((TOK, 128), BF16)
        tops[64 * h : 64 * h + 64, :] = jnp.broadcast_to(sinks_ref[h], (TOK, 128))
    normed_ref[:, D:] = jnp.zeros((TOK, DP - D), BF16)

    def attend(names, part, first=False):
        where = [kv_index(*name) for name in names]
        lane = iota((TOK, 256), 1)
        owner = jnp.where(lane < 128, jnp.where(lane < 64, where[0], where[1]), jnp.where(lane < 192, where[2], where[3]))
        bias = jnp.where(owner * TOK + (lane & 63) <= ctx * TOK + iota((TOK, 256), 0), 0.0, -1e30)

        def rows(i, _):
            r = pl.multiple_of(i * 512, 512)
            key_block = jnp.concatenate([kv[w, :, 0:256] for w in where], axis=0)
            value_block = jnp.concatenate([kv[w, :, 256:512] for w in where], axis=0)
            scores = lax.dot_general(
                qz[pl.ds(r, 512), :], key_block, (((1,), (1,)), ((), ())), preferred_element_type=F32)
            scores = (scores.reshape(8, TOK, 256) + bias[None]).reshape(512, 256)
            old = tops[pl.ds(r, 512), :1]
            top = jnp.maximum(jnp.max(scores, axis=1, keepdims=True), old)
            prob = jnp.exp(scores - top)
            shrink = jnp.exp(old - top)
            added = jnp.sum(prob, axis=1, keepdims=True)
            value = dot(prob.astype(BF16), value_block)
            tops[pl.ds(r, 512), :] = jnp.broadcast_to(top, (512, 128))
            if first:
                totals[pl.ds(r, 512), :] = jnp.broadcast_to(shrink + added, (512, 128))
                heads[pl.ds(r, 512), :] = value
            else:
                totals[pl.ds(r, 512), :] = totals[pl.ds(r, 512), :] * shrink + added
                heads[pl.ds(r, 512), :] = heads[pl.ds(r, 512), :] * shrink + value
            return 0

        lax.fori_loop(2 * part, 2 * part + 2, rows, 0)

    def take(*names):
        for name in names:
            kv_gather.take(*name)

    chunks = [
        (("A", 0), ("A", 1), ("A", -1), ("B", 0)), (("A", 2), ("A", -2), ("B", 1), ("B", -1)),
        (("A", 3), ("A", -3), ("B", 2), ("B", -2)), (("A", 4), ("B", 3), ("B", -3), ("B", 4)),
    ]
    take(*chunks[0][1:])
    ow_gather.ring(1, 0)
    attend(chunks[0], 0, True)
    ow_gather.ring(1, 1)
    take(("A", 2), ("A", -2))
    attend(chunks[0], 1, True)
    ow_gather.other(0, 0)
    ow_gather.other(0, 1)
    take(("B", 1), ("B", -1))
    ow_gather.ring(2, 0)
    take(("A", 3), ("A", -3))
    ow_gather.near(1, 0)
    ow_gather.near(1, 1)
    attend(chunks[1], 0)
    ow_gather.ring(2, 1)
    take(("B", 2), ("B", -2))
    attend(chunks[1], 1)
    take(("A", 4),)
    ow_gather.ring(3, 0)
    ow_gather.near(2, 0)
    attend(chunks[2], 0)
    ow_gather.near(2, 1)
    attend(chunks[2], 1)
    ow_gather.far(1, 0)
    ow_gather.far(1, 1)
    ow_gather.ring(3, 1)
    take(("B", 3), ("B", -3), ("B", 4))
    ow_gather.near(3, 0)
    attend(chunks[3], 0)
    ow_gather.ring(4, 0)
    ow_gather.ring(4, 1)
    attend(chunks[3], 1)
    ow_gather.near(3, 1)
    for half in range(2):
        ow_gather.far(2, half)

    for m in range(QH // 2):
        g = m // 4
        pair = []
        for h in (2 * m, 2 * m + 1):
            tile = heads[64 * h : 64 * h + 64, 128 * (g // 2) : 128 * (g // 2) + 128]
            tile = tile / totals[64 * h : 64 * h + 64, :]
            pair.append(pltpu.roll(tile, 64, 1) if h % 2 != g % 2 else tile)
        attended[m] = jnp.where(left, pair[0], pair[1]).astype(BF16)

    def project(blocks):
        chips = [(x_hi if side == "A" else 1 - x_hi) * 8 + ((z - step + 8) & 7) for side, step in blocks]
        return dot(
            jnp.concatenate([attended[m] for m in chips], axis=1),
            jnp.concatenate([wbuf[pl.ds(4 * m, 4)].reshape(128, D) for m in chips], axis=0))

    for name in (("A", 0), ("A", 1), ("A", -1), ("A", 2), ("A", -2), ("B", 0), ("near", 1), ("far", 1)):
        for copy in ow_gather.given_by[name]:
            copy.wait_recv()
    branch = project([("A", 0), ("A", 1), ("A", -1), ("A", 2), ("A", -2), ("B", 0), ("B", 1), ("B", -1)])
    for half in range(2):
        ow_gather.far(3, half)
        ow_gather.other(4, half)
    for name in (("A", 3), ("A", -3), ("A", 4), ("near", 2), ("far", 2), ("near", 3), ("far", 3), ("B", 4)):
        for copy in ow_gather.given_by[name]:
            copy.wait_recv()
    branch = branch + project(
        [("A", 3), ("A", -3), ("A", 4), ("B", 2), ("B", -2), ("B", 3), ("B", -3), ("B", 4)])
    branch_ref[...] = branch
    mean_sq = jnp.sum(branch * branch, axis=1, keepdims=True) * (1.0 / D)
    normed_ref[:, :D] = (branch * lax.rsqrt(mean_sq + 1e-05) * gain_ref[...].reshape(1, D)).astype(BF16)

    routes_t = routes_t_ref[...]
    expert = offset_expert(iota((CHIPS, TOK), 0), x_hi, z)
    hit = jnp.zeros((CHIPS, TOK), F32)
    for k in range(TOPK):
        hit = hit + (routes_t[k : k + 1, :] == expert).astype(F32)
    before = (iota((TOK, 256), 0) < (iota((TOK, 256), 1) & 63)).astype(BF16)
    same = (iota((TOK, 256), 0) == (iota((TOK, 256), 1) & 63)).astype(BF16)
    hit16 = hit.astype(BF16)
    slot4 = dot(hit16, before)
    hit4 = dot(hit16, same)
    slot4 = jnp.where(hit4 > 0.5, slot4, -1000.0)
    slot_i = slot4.astype(jnp.int32)
    slot_main = slot_i[:, :TOK]
    pick = (jnp.broadcast_to(slot_main[:, None, :], (CHIPS, 16, TOK)) == iota((CHIPS, 16, TOK), 1)).astype(F32)
    pick = pick.astype(BF16).reshape(CHIPS * 16, TOK)
    rows = dot(pick, normed_ref[...]).astype(BF16)
    for j in range(12):
        send[:, 16 * j : 16 * j + 16, :] = rows[:, 128 * j : 128 * j + 128].reshape(CHIPS, 16, 128)
    tail_key = jnp.where(slot_i >= 16, slot_i - 16 + 4 * (iota((CHIPS, 256), 1) >> 6), -1)
    tail = (jnp.broadcast_to(tail_key[:, None, :], (CHIPS, 16, 256)) == iota((CHIPS, 16, 256), 1)).astype(F32)
    tail = tail.astype(BF16).reshape(CHIPS * 16, 256)
    for g in range(3):
        stacked = jnp.concatenate([normed_ref[:, 128 * (4 * g + j) : 128 * (4 * g + j + 1)] for j in range(4)], axis=0)
        send[:, 192 + 16 * g : 208 + 16 * g, :] = dot(tail, stacked).astype(BF16).reshape(CHIPS, 16, 128)

    outgoing = {}
    for i in reversed(range(1, CHIPS)):
        copy = pltpu.make_async_remote_copy(
            src_ref=send.at[i], dst_ref=mine.at[i], send_sem=send_sem.at[i], recv_sem=mine_sem.at[i],
            device_id=peer(i), device_id_type=MESH)
        copy.start()
        outgoing[i] = copy

    def forward(i):
        copy = pltpu.make_async_remote_copy(
            src_ref=send.at[0] if i == 0 else mine.at[i], dst_ref=other.at[i],
            send_sem=fwd_sem.at[i], recv_sem=other_sem.at[i],
            device_id=partner, device_id_type=MESH)
        copy.start()
        return copy

    forwards = {0: forward(0)}

    def arrive(c):
        for i in reversed(range(max(1, GROUP * c), GROUP * (c + 1))):
            outgoing[i].wait_recv()
            forwards[i] = forward(i)


    padded = jnp.concatenate(
        [routes_t.astype(F32), gates_t_ref[...]], axis=0)
    padded = jnp.transpose(jnp.concatenate([padded, jnp.zeros((8, 64), F32)], axis=1))[:TOK, :]
    routes = padded[:, :TOPK].astype(jnp.int32)
    gates = padded[:, TOPK:]
    expert_of = offset_expert(iota((TOK, CHIPS), 1), x_hi, z)
    hits = jnp.zeros((TOK, CHIPS), F32)
    for k in range(TOPK):
        hits = hits + (routes[:, k : k + 1] == expert_of).astype(F32)
    earlier = (iota((TOK, TOK), 1) < iota((TOK, TOK), 0)).astype(BF16)
    slots = jnp.where(hits > 0.5, dot(earlier, hits.astype(BF16)), 100.0)
    spread = (iota((CHIPS, 256), 0) == (iota((CHIPS, 256), 1) >> 4)).astype(BF16)
    slots = dot(slots.astype(BF16), spread).astype(jnp.int32)
    column_expert = offset_expert(iota((TOK, 256), 1) >> 4, x_hi, z)
    weight = jnp.zeros((TOK, 256), F32)
    for k in range(TOPK):
        weight = weight + jnp.where(routes[:, k : k + 1] == column_expert, gates[:, k : k + 1], 0.0)
    place = iota((TOK, 256), 1) & 15
    combine_main = jnp.concatenate(split3(jnp.where(slots == place, weight, 0.0)), axis=0)
    combine_tail = [
        jnp.concatenate(split3(jnp.where((slots - 16 == (place & 3)) & ((place >> 2) == j), weight, 0.0)), axis=0)
        for j in range(4)
    ]

    wide = iota((512, 512), 0)
    perm[:512, :] = (iota((512, 512), 1) == 4 * (wide & 127) + (wide >> 7)).astype(F32).astype(BF16)
    narrow = iota((256, 512), 0)
    perm[512:768, :] = (iota((256, 512), 1) == 4 * (narrow & 63) + (narrow >> 6)).astype(F32).astype(BF16)
    wg[D:, :] = jnp.zeros((DP - D, FF), BF16)
    wu[D:, :] = jnp.zeros((DP - D, FF), BF16)
    wd[:, D:] = jnp.zeros((FF, DP - D), BF16)
    loads[3].wait()
    turn(gct, gc, D, 192)
    code_planes(gc, planes, D, 192)
    weight_rows(planes, gs, perm, wg, D, 192, 288)
    loads[4].wait()
    turn(uct, uc, D, 192)
    code_planes(uc, planes, D, 192)
    weight_rows(planes, us, perm, wu, D, 192, 288)
    loads[5].wait()
    turn(dct, dc, FF, 360)
    code_planes(dc, planes, FF, 360)
    arrive(CHIPS // GROUP - 1)
    weight_rows(planes, ds, perm, wd, FF, 360, 256)

    side = 32 * GROUP
    a, b = iota((side, side), 0), iota((side, side), 1)
    moved_to = lambda r: ((r >> 2) % (2 * GROUP)) * 16 + (r // (8 * GROUP)) * 4 + (r & 3)
    to_rows = (b == moved_to(a)).astype(F32).astype(BF16)
    to_block = (a == moved_to(b)).astype(F32).astype(BF16)

    sent_pieces = {}
    sent_results = []

    def finish(c):
        sent_pieces[c].wait_recv()
        for i in range(GROUP * c, GROUP * (c + 1)):
            total = (p_mine[i].astype(F32) + p_in[i].astype(F32)).astype(BF16)
            if i == 0:
                ret[0] = total
            else:
                result[i] = total
        for i in reversed(range(max(1, GROUP * c), GROUP * (c + 1))):
            copy = pltpu.make_async_remote_copy(
                src_ref=result.at[i], dst_ref=ret.at[i], send_sem=res_sem.at[i], recv_sem=ret_sem.at[i],
                device_id=source(i), device_id_type=MESH)
            copy.start()
            sent_results.append(copy)

    for c in reversed(range(CHIPS // GROUP)):
        if c < CHIPS // GROUP - 1:
            arrive(c)
        for i in range(GROUP * c, GROUP * (c + 1)):
            forwards[i].wait_recv()
        if c == 0:
            mine[0] = send[0]

        def both(lo, hi):
            return jnp.concatenate(
                [ref[GROUP * c : GROUP * (c + 1), lo:hi, :].reshape(16 * GROUP, 128) for ref in (mine, other)],
                axis=0)

        main = jnp.concatenate([both(16 * j, 16 * j + 16) for j in range(12)], axis=1)
        tails = []
        for g in range(3):
            moved = dot(to_rows, both(192 + 16 * g, 208 + 16 * g)).astype(BF16)
            tails += [moved[8 * GROUP * j : 8 * GROUP * (j + 1), :] for j in range(4)]
        x = jnp.concatenate([main, jnp.concatenate(tails, axis=1)], axis=0)
        gate_act = dot(x, wg[...])
        up_act = dot(x, wu[...])
        active = ((up_act + 1.0) * gate_act * jax.nn.sigmoid(1.702 * gate_act)).astype(BF16)
        y = dot(active, wd[...]).astype(BF16)
        for j in range(12):
            tile = y[:side, 128 * j : 128 * j + 128]
            p_mine[GROUP * c : GROUP * (c + 1), 16 * j : 16 * j + 16, :] = tile[: side // 2].reshape(GROUP, 16, 128)
            p_other[GROUP * c : GROUP * (c + 1), 16 * j : 16 * j + 16, :] = tile[side // 2 :].reshape(GROUP, 16, 128)
        for g in range(3):
            tiles = jnp.concatenate([y[side:, 128 * (4 * g + j) : 128 * (4 * g + j + 1)] for j in range(4)], axis=0)
            back = dot(to_block, tiles).astype(BF16)
            p_mine[GROUP * c : GROUP * (c + 1), 192 + 16 * g : 208 + 16 * g, :] = back[: side // 2].reshape(GROUP, 16, 128)
            p_other[GROUP * c : GROUP * (c + 1), 192 + 16 * g : 208 + 16 * g, :] = back[side // 2 :].reshape(GROUP, 16, 128)
        copy = pltpu.make_async_remote_copy(
            src_ref=p_other.at[pl.ds(GROUP * c, GROUP)], dst_ref=p_in.at[pl.ds(GROUP * c, GROUP)],
            send_sem=pout_sem.at[c], recv_sem=pin_sem.at[c], device_id=partner, device_id_type=MESH)
        copy.start()
        sent_pieces[c] = copy
        finish(c)

    for copy in sent_results:
        copy.wait_recv()
    for j in range(12):
        part = dot(combine_main, ret[:, 16 * j : 16 * j + 16, :].reshape(256, 128))
        g = j // 4
        part = part + dot(combine_tail[j % 4], ret[:, 192 + 16 * g : 208 + 16 * g, :].reshape(256, 128))
        mixed = part[:TOK] + part[TOK : 2 * TOK] + part[2 * TOK :]
        lo, hi = 128 * j, min(128 * j + 128, D)
        out_ref[:, lo:hi] = branch_ref[:, lo:hi] + mixed[:, : hi - lo]

    for copy in list(outgoing.values()) + list(forwards.values()) + list(sent_pieces.values()) + sent_results + kv_gather.copies + ow_gather.copies + ow_gather.given:
        copy.wait_send()


def local(
    queries, keys, values, sinks, out_weight, norm_gain, routes, gates,
    gate_codes, up_codes, down_codes, gate_scales, up_scales, down_scales,
):
    vmem = pl.BlockSpec(memory_space=pltpu.VMEM)
    hbm = pl.BlockSpec(memory_space=pl.ANY)
    dma = pltpu.SemaphoreType.DMA
    blocks = pltpu.VMEM((CHIPS, BLK, 128), BF16)
    out = pl.pallas_call(
        layer_kernel,
        out_shape=jax.ShapeDtypeStruct((TOK, D), F32),
        in_specs=[hbm] * 3 + [pl.BlockSpec(memory_space=pltpu.SMEM), hbm] + [vmem] * 3 + [hbm] * 3 + [vmem] * 3,
        out_specs=vmem,
        scratch_shapes=[
            pltpu.VMEM((TOK, QH * HD), BF16),
            pltpu.VMEM((16, TOK, 512), BF16),
            pltpu.VMEM((QH * TOK, 256), BF16),
            pltpu.VMEM((QH * TOK, 128), F32),
            pltpu.VMEM((QH * TOK, 128), F32),
            pltpu.VMEM((QH * TOK, 256), F32),
            pltpu.VMEM((QH // 2, TOK, 128), BF16),
            pltpu.VMEM((64, 32, D), BF16),
            pltpu.VMEM((TOK, D), F32),
            pltpu.VMEM((TOK, DP), BF16),
            pltpu.VMEM((192, D), jnp.int32),
            pltpu.VMEM((192, D), jnp.int32),
            pltpu.VMEM((360, FF), jnp.int32),
            pltpu.VMEM((D, 192), jnp.int32),
            pltpu.VMEM((D, 192), jnp.int32),
            pltpu.VMEM((FF, 360), jnp.int32),
            pltpu.VMEM((D, DP), BF16),
            pltpu.VMEM((FF, 512), BF16),
            pltpu.VMEM((DP, FF), BF16),
            pltpu.VMEM((DP, FF), BF16),
            pltpu.VMEM((FF, DP), BF16),
            blocks, blocks, blocks, blocks, blocks, blocks, blocks, blocks,
            dma((7,)), dma((15,)), dma((15,)), dma((30,)), dma((30,)), dma((32,)), dma((32,)),
            dma((CHIPS,)), dma((CHIPS,)), dma((CHIPS,)), dma((CHIPS,)), dma((CHIPS // GROUP,)), dma((CHIPS // GROUP,)),
            dma((CHIPS,)), dma((CHIPS,)),
        ],
        compiler_params=pltpu.CompilerParams(collective_id=0, has_side_effects=True, vmem_limit_bytes=60 * 1024 * 1024),
        name="layer",
    )(
        queries[0], keys[0], values[0], sinks, out_weight.reshape(2, 32, D), norm_gain, routes[0].T, gates[0].T,
        gate_codes[0].T, up_codes[0].T, down_codes[0].T, jnp.swapaxes(gate_scales, 0, 1), jnp.swapaxes(up_scales, 0, 1), down_scales[0],
    )
    return out.astype(BF16)[None]


def solution(mesh):
    return jax.shard_map(
        local,
        mesh=mesh,
        in_specs=(
            P("exp", "ctx", None),
            P("exp", "ctx", None),
            P("exp", "ctx", None),
            P(),
            P("exp", None),
            P(),
            P("exp", "ctx", None),
            P("exp", "ctx", None),
            P("exp", None, None),
            P("exp", None, None),
            P("exp", None, None),
            P("exp", None, None),
            P("exp", None, None),
            P("exp", None, None),
        ),
        out_specs=P("exp", "ctx", None),
        check_vma=False,
    )
```

```python
import functools
import math

import jax
import jax.numpy as jnp
from jax import lax
from jax.experimental import pallas as pl
from jax.experimental.pallas import tpu as pltpu
from jax.sharding import PartitionSpec as P

QH = 32
KVH = 4
HD = 64
TOPK = 4
D = 1440
DP = 1536
FF = 768
TOK = 64
CHIPS = 16
BLK = 240
GROUP = 4
MESH = pl.DeviceIdType.MESH
F32 = jnp.float32
BF16 = jnp.bfloat16

OFFSETS = []
for step in range(8):
    half = (step + 1) // 2
    dz = half if step % 2 else -half
    OFFSETS += [(0, dz), (1, dz)]


def iota(shape, axis):
    return lax.broadcasted_iota(jnp.int32, shape, axis)


def dot(a, b):
    return jnp.dot(a, b, preferred_element_type=F32)


def offset_expert(i, x_hi, z):
    step = i >> 1
    half = (step + 1) >> 1
    dz = jnp.where((step & 1) == 1, half, -half)
    return ((x_hi + (i & 1)) & 1) * 8 + ((z + dz + 8) & 7)


def split3(x):
    hi = x.astype(BF16)
    rest = x - hi.astype(F32)
    mid = rest.astype(BF16)
    low = (rest - mid.astype(F32)).astype(BF16)
    return hi, mid, low


def fp4_plane(words, shift):
    code = (words >> shift) & 15
    size = code & 7
    twice = size + jnp.maximum(size - 4, 0) + 2 * jnp.maximum(size - 6, 0)
    return jnp.where(code >= 8, -twice, twice).astype(F32).astype(BF16)


def turn(source_ref, target_ref, rows, words):
    for lo in range(0, rows, 128):
        hi = min(lo + 128, rows)
        target_ref[lo:hi, :] = jnp.transpose(source_ref[:, lo:hi])


def code_planes(codes_ref, planes_ref, rows, words):
    blocks = [(b, 128 * b, min(128, words - 128 * b)) for b in range((words + 127) // 128)]

    def step(i, _):
        r = pl.multiple_of(i * 32, 32)
        for b, lo, count in blocks:
            w = codes_ref[pl.ds(r, 32), lo : lo + count]
            if count == 64:
                w = jnp.concatenate([w, w], axis=1)
                shifts = [(iota((32, 128), 1) >> 6) * 4 + 8 * k for k in range(2)]
            else:
                if count < 128:
                    w = jnp.concatenate([w, jnp.zeros((32, 128 - count), jnp.int32)], axis=1)
                shifts = [4 * k for k in range(4)]
            for k, shift in enumerate(shifts):
                at = 512 * b + 128 * k
                planes_ref[pl.ds(r, 32), at : at + 128] = fp4_plane(w, shift)
        return 0

    lax.fori_loop(0, rows // 32, step, 0)


def weight_rows(planes_ref, scales_ref, perm_ref, out_ref, rows, words, m_rows):
    groups = m_rows // 32
    blocks = [(b, min(128, words - 128 * b)) for b in range((words + 127) // 128)]
    for i in range(rows // m_rows):
        r = i * m_rows
        for b, count in blocks:
            width = 4 * count
            if count == 64:
                value = dot(planes_ref[r : r + m_rows, 512 * b : 512 * b + 256], perm_ref[512:768, :256])
            else:
                value = dot(planes_ref[r : r + m_rows, 512 * b : 512 * b + 512], perm_ref[:512, :])
            value = value[:, :width]
            scale = scales_ref[groups * i : groups * (i + 1), ..., 512 * b : 512 * b + width]
            factor = (1 << (scale - 118)).astype(F32) * (2.0**-10)
            for n in range(groups):
                piece = value[32 * n : 32 * n + 32] * (factor[n] if factor.ndim == 3 else factor[n : n + 1])
                out_ref[r + 32 * n : r + 32 * n + 32, 512 * b : 512 * b + width] = piece.astype(BF16)


class Gather:
    RELAYS = {
        ("A", 1): "+", ("A", 2): "+s", ("A", 3): "+s", ("A", 4): "s",
        ("A", -1): "-", ("A", -2): "-", ("A", -3): "s",
        ("B", 0): "+-", ("B", -1): "-",
    }

    def __init__(self, buf, index, sends, recvs, there):
        self.buf, self.index, self.sends, self.recvs = buf, index, sends, recvs
        self.there = there
        self.count = 0
        self.waits = {}
        self.copies = []

    def send(self, way, side, step):
        where = self.index(side, step)
        if way == "+":
            name = (side, step + 1)
        elif way == "-":
            name = (side, step - 1)
        else:
            name = ("B", step)
        copy = pltpu.make_async_remote_copy(
            src_ref=self.buf.at[where], dst_ref=self.buf.at[where], send_sem=self.sends.at[self.count],
            recv_sem=self.recvs.at[self.count], device_id=self.there[way], device_id_type=MESH)
        copy.start()
        self.count += 1
        self.copies.append(copy)
        self.waits[name] = copy

    def begin(self):
        for way in "+-s":
            self.send(way, "A", 0)

    def take(self, side, step):
        self.waits[side, step].wait_recv()
        for way in self.RELAYS.get((side, step), ""):
            self.send(way, side, step)


class WeightGather:
    def __init__(self, buf, unit, turn, there, partner, sems):
        self.buf, self.unit, self.sign, self.there, self.partner = buf, unit, turn, there, partner
        self.sends, self.recvs, self.give_sends, self.give_recvs = sems
        self.copies, self.given, self.by_name, self.given_by = [], [], {}, {}

    def send(self, name, way, side, step, half):
        where = self.unit(side, step, half)
        n = len(self.copies)
        copy = pltpu.make_async_remote_copy(
            src_ref=self.buf.at[where], dst_ref=self.buf.at[where], send_sem=self.sends.at[n],
            recv_sem=self.recvs.at[n], device_id=self.there[way], device_id_type=MESH)
        copy.start()
        self.copies.append(copy)
        self.by_name[name + (half,)] = copy

    def give(self, name, side, step, half):
        where = self.unit(side, step, half)
        n = len(self.given)
        copy = pltpu.make_async_remote_copy(
            src_ref=self.buf.at[where], dst_ref=self.buf.at[where], send_sem=self.give_sends.at[n],
            recv_sem=self.give_recvs.at[n], device_id=self.partner, device_id_type=MESH)
        copy.start()
        self.given.append(copy)
        self.given_by[name] = self.given_by.get(name, []) + [copy]

    def begin(self):
        for half in range(2):
            self.send(("A", 1), "+", "A", 0, half)
            self.send(("A", -1), "-", "A", 0, half)
            self.send(("B", 0), "cross", "A", 0, half)
        for half in range(2):
            self.give(("A", 0), "A", 0, half)

    def ring(self, k, half):
        ways = [1, -1] if k < 4 else [1 if half == 0 else -1]
        for way in ways:
            self.by_name["A", way * k, half].wait_recv()
        for way in ways:
            if k < 3 or (k == 3 and (half == 0) == (way == 1)):
                self.send(("A", way * (k + 1)), "+" if way == 1 else "-", "A", way * k, half)
        if k < 4:
            self.send(("B", "near", k), "cross", "A", -self.sign * k, half)
        else:
            self.send(("B", 4), "cross", "A", 4, half)
        for way in ways:
            self.give(("A", way * k if k < 4 else 4), "A", way * k, half)

    def near(self, k, half):
        self.by_name["B", "near", k, half].wait_recv()
        self.send(("B", "far", k), "pair", "B", self.sign * k, half)
        self.give(("near", k), "B", self.sign * k, half)

    def far(self, k, half):
        self.by_name["B", "far", k, half].wait_recv()
        self.give(("far", k), "B", -self.sign * k, half)

    def other(self, k, half):
        self.by_name["B", k, half].wait_recv()
        self.give(("B", k), "B", k, half)


def layer_kernel(
    queries_hbm, keys_hbm, values_hbm, sinks_ref, ow_hbm, gain_ref, routes_t_ref, gates_t_ref,
    gc_hbm, uc_hbm, dc_hbm, gs, us, ds,
    out_ref,
    q_in, kv, qz, tops, totals, heads, attended, wbuf, branch_ref, normed_ref,
    gct, uct, dct, gc, uc, dc, planes, perm, wg, wu, wd,
    send, mine, other, p_mine, p_other, p_in, result, ret,
    in_sem, kv_send, kv_recv, ow_send, ow_recv, give_send, give_recv,
    send_sem, mine_sem, fwd_sem, other_sem, pout_sem, pin_sem, res_sem, ret_sem,
):
    me = lax.axis_index("exp")
    ctx = lax.axis_index("ctx")
    core = me & 1
    z = (me >> 1) & 7
    x_hi = me >> 4
    y = ctx >> 1
    x_lo = ctx & 1

    def peer(i):
        dx, dz = OFFSETS[i]
        return {"exp": (((x_hi + dx) & 1) * 8 + ((z + dz + 8) & 7)) * 2 + core, "ctx": ctx ^ dx}

    def source(i):
        dx, dz = OFFSETS[i]
        return {"exp": (((x_hi + dx) & 1) * 8 + ((z - dz + 8) & 7)) * 2 + core, "ctx": ctx ^ dx}

    partner = {"exp": me ^ 1}
    kv_there = {
        "+": {"ctx": ((y + 1) & 7) * 2 + x_lo}, "-": {"ctx": ((y + 7) & 7) * 2 + x_lo}, "s": {"ctx": ctx ^ 1},
    }
    ow_there = {
        "+": {"exp": (x_hi * 8 + ((z + 1) & 7)) * 2 + core}, "-": {"exp": (x_hi * 8 + ((z + 7) & 7)) * 2 + core},
        "cross": {"ctx": ctx ^ 1, "exp": me ^ 16}, "pair": {"ctx": ctx ^ 1},
    }

    def kv_index(side, step):
        return ((y - step + 8) & 7) * 2 + (x_lo if side == "A" else 1 - x_lo)

    def ow_unit(side, step, half):
        return (((x_hi if side == "A" else 1 - x_hi) * 8 + ((z - step + 8) & 7)) * 2 + core) * 2 + half

    kv_gather = Gather(kv, kv_index, kv_send, kv_recv, kv_there)
    ow_gather = WeightGather(
        wbuf, ow_unit, 1 - 2 * x_lo, ow_there, partner, (ow_send, ow_recv, give_send, give_recv))

    barrier = pltpu.get_barrier_semaphore()
    greeted = [peer(i) for i in range(1, CHIPS)] + [partner, kv_there["+"], kv_there["-"], kv_there["s"]]
    for device in greeted:
        pl.semaphore_signal(barrier, inc=1, device_id=device, device_id_type=MESH)

    loads = []
    for n, (src, dst) in enumerate((
        (keys_hbm, kv.at[ctx, :, 0:256]), (values_hbm, kv.at[ctx, :, 256:512]), (ow_hbm, wbuf.at[pl.ds(2 * me, 2)]),
        (gc_hbm, gct), (uc_hbm, uct), (dc_hbm, dct), (queries_hbm, q_in),
    )):
        copy = pltpu.make_async_copy(src, dst, in_sem.at[n])
        copy.start()
        loads.append(copy)
    loads[0].wait()
    loads[1].wait()
    loads[2].wait()
    pl.semaphore_wait(barrier, len(greeted))
    kv_gather.begin()
    ow_gather.begin()

    loads[6].wait()
    left = iota((TOK, 128), 1) < 64
    for h in range(QH):
        g = h // 8
        tile = q_in[:, 128 * (h // 2) : 128 * (h // 2) + 128].astype(F32) * (1.0 / math.sqrt(HD))
        if h % 2 != g % 2:
            tile = pltpu.roll(tile, 64, 1)
        tile = jnp.where(left if g % 2 == 0 else ~left, tile, 0.0).astype(BF16)
        lo = 128 * (g // 2)
        qz[64 * h : 64 * h + 64, lo : lo + 128] = tile
        qz[64 * h : 64 * h + 64, 128 - lo : 256 - lo] = jnp.zeros((TOK, 128), BF16)
        tops[64 * h : 64 * h + 64, :] = jnp.broadcast_to(sinks_ref[h], (TOK, 128))
    normed_ref[:, D:] = jnp.zeros((TOK, DP - D), BF16)

    def attend(names, part, first=False):
        where = [kv_index(*name) for name in names]
        lane = iota((TOK, 256), 1)
        owner = jnp.where(lane < 128, jnp.where(lane < 64, where[0], where[1]), jnp.where(lane < 192, where[2], where[3]))
        bias = jnp.where(owner * TOK + (lane & 63) <= ctx * TOK + iota((TOK, 256), 0), 0.0, -1e30)

        def rows(i, _):
            r = pl.multiple_of(i * 512, 512)
            key_block = jnp.concatenate([kv[w, :, 0:256] for w in where], axis=0)
            value_block = jnp.concatenate([kv[w, :, 256:512] for w in where], axis=0)
            scores = lax.dot_general(
                qz[pl.ds(r, 512), :], key_block, (((1,), (1,)), ((), ())), preferred_element_type=F32)
            scores = (scores.reshape(8, TOK, 256) + bias[None]).reshape(512, 256)
            old = tops[pl.ds(r, 512), :1]
            top = jnp.maximum(jnp.max(scores, axis=1, keepdims=True), old)
            prob = jnp.exp(scores - top)
            shrink = jnp.exp(old - top)
            added = jnp.sum(prob, axis=1, keepdims=True)
            value = dot(prob.astype(BF16), value_block)
            tops[pl.ds(r, 512), :] = jnp.broadcast_to(top, (512, 128))
            if first:
                totals[pl.ds(r, 512), :] = jnp.broadcast_to(shrink + added, (512, 128))
                heads[pl.ds(r, 512), :] = value
            else:
                totals[pl.ds(r, 512), :] = totals[pl.ds(r, 512), :] * shrink + added
                heads[pl.ds(r, 512), :] = heads[pl.ds(r, 512), :] * shrink + value
            return 0

        lax.fori_loop(2 * part, 2 * part + 2, rows, 0)

    def take(*names):
        for name in names:
            kv_gather.take(*name)

    chunks = [
        (("A", 0), ("A", 1), ("A", -1), ("B", 0)), (("A", 2), ("A", -2), ("B", 1), ("B", -1)),
        (("A", 3), ("A", -3), ("B", 2), ("B", -2)), (("A", 4), ("B", 3), ("B", -3), ("B", 4)),
    ]
    take(*chunks[0][1:])
    ow_gather.ring(1, 0)
    attend(chunks[0], 0, True)
    ow_gather.ring(1, 1)
    take(("A", 2), ("A", -2))
    attend(chunks[0], 1, True)
    ow_gather.other(0, 0)
    ow_gather.other(0, 1)
    take(("B", 1), ("B", -1))
    ow_gather.ring(2, 0)
    take(("A", 3), ("A", -3))
    ow_gather.near(1, 0)
    ow_gather.near(1, 1)
    attend(chunks[1], 0)
    ow_gather.ring(2, 1)
    take(("B", 2), ("B", -2))
    attend(chunks[1], 1)
    take(("A", 4),)
    ow_gather.ring(3, 0)
    ow_gather.near(2, 0)
    attend(chunks[2], 0)
    ow_gather.near(2, 1)
    attend(chunks[2], 1)
    ow_gather.far(1, 0)
    ow_gather.far(1, 1)
    ow_gather.ring(3, 1)
    take(("B", 3), ("B", -3), ("B", 4))
    ow_gather.near(3, 0)
    attend(chunks[3], 0)
    ow_gather.ring(4, 0)
    ow_gather.ring(4, 1)
    attend(chunks[3], 1)
    ow_gather.near(3, 1)
    for half in range(2):
        ow_gather.far(2, half)

    for m in range(QH // 2):
        g = m // 4
        pair = []
        for h in (2 * m, 2 * m + 1):
            tile = heads[64 * h : 64 * h + 64, 128 * (g // 2) : 128 * (g // 2) + 128]
            tile = tile / totals[64 * h : 64 * h + 64, :]
            pair.append(pltpu.roll(tile, 64, 1) if h % 2 != g % 2 else tile)
        attended[m] = jnp.where(left, pair[0], pair[1]).astype(BF16)

    def project(blocks):
        chips = [(x_hi if side == "A" else 1 - x_hi) * 8 + ((z - step + 8) & 7) for side, step in blocks]
        return dot(
            jnp.concatenate([attended[m] for m in chips], axis=1),
            jnp.concatenate([wbuf[pl.ds(4 * m, 4)].reshape(128, D) for m in chips], axis=0))

    routes_t = routes_t_ref[...]
    expert = offset_expert(iota((CHIPS, TOK), 0), x_hi, z)
    hit = jnp.zeros((CHIPS, TOK), F32)
    for k in range(TOPK):
        hit = hit + (routes_t[k : k + 1, :] == expert).astype(F32)
    before = (iota((TOK, 256), 0) < (iota((TOK, 256), 1) & 63)).astype(BF16)
    same = (iota((TOK, 256), 0) == (iota((TOK, 256), 1) & 63)).astype(BF16)
    hit16 = hit.astype(BF16)
    slot4 = dot(hit16, before)
    hit4 = dot(hit16, same)
    slot4 = jnp.where(hit4 > 0.5, slot4, -1000.0)
    slot_i = slot4.astype(jnp.int32)
    slot_main = slot_i[:, :TOK]
    pick = (jnp.broadcast_to(slot_main[:, None, :], (CHIPS, 16, TOK)) == iota((CHIPS, 16, TOK), 1)).astype(F32)
    pick = pick.astype(BF16).reshape(CHIPS * 16, TOK)
    tail_key = jnp.where(slot_i >= 16, slot_i - 16 + 4 * (iota((CHIPS, 256), 1) >> 6), -1)
    tail = (jnp.broadcast_to(tail_key[:, None, :], (CHIPS, 16, 256)) == iota((CHIPS, 16, 256), 1)).astype(F32)
    tail = tail.astype(BF16).reshape(CHIPS * 16, 256)

    for name in (("A", 0), ("A", 1), ("A", -1), ("A", 2), ("A", -2), ("B", 0), ("near", 1), ("far", 1)):
        for copy in ow_gather.given_by[name]:
            copy.wait_recv()
    branch = project([("A", 0), ("A", 1), ("A", -1), ("A", 2), ("A", -2), ("B", 0), ("B", 1), ("B", -1)])
    for half in range(2):
        ow_gather.far(3, half)
        ow_gather.other(4, half)
    for name in (("A", 3), ("A", -3), ("A", 4), ("near", 2), ("far", 2), ("near", 3), ("far", 3), ("B", 4)):
        for copy in ow_gather.given_by[name]:
            copy.wait_recv()
    branch = branch + project(
        [("A", 3), ("A", -3), ("A", 4), ("B", 2), ("B", -2), ("B", 3), ("B", -3), ("B", 4)])
    branch_ref[...] = branch
    mean_sq = jnp.sum(branch * branch, axis=1, keepdims=True) * (1.0 / D)
    normed_ref[:, :D] = (branch * lax.rsqrt(mean_sq + 1e-05) * gain_ref[...].reshape(1, D)).astype(BF16)

    rows = dot(pick, normed_ref[...]).astype(BF16)
    for j in range(12):
        send[:, 16 * j : 16 * j + 16, :] = rows[:, 128 * j : 128 * j + 128].reshape(CHIPS, 16, 128)
    for g in range(3):
        stacked = jnp.concatenate([normed_ref[:, 128 * (4 * g + j) : 128 * (4 * g + j + 1)] for j in range(4)], axis=0)
        send[:, 192 + 16 * g : 208 + 16 * g, :] = dot(tail, stacked).astype(BF16).reshape(CHIPS, 16, 128)

    outgoing = {}
    for i in reversed(range(1, CHIPS)):
        copy = pltpu.make_async_remote_copy(
            src_ref=send.at[i], dst_ref=mine.at[i], send_sem=send_sem.at[i], recv_sem=mine_sem.at[i],
            device_id=peer(i), device_id_type=MESH)
        copy.start()
        outgoing[i] = copy

    def forward(i):
        copy = pltpu.make_async_remote_copy(
            src_ref=send.at[0] if i == 0 else mine.at[i], dst_ref=other.at[i],
            send_sem=fwd_sem.at[i], recv_sem=other_sem.at[i],
            device_id=partner, device_id_type=MESH)
        copy.start()
        return copy

    forwards = {0: forward(0)}

    def arrive(c):
        for i in reversed(range(max(1, GROUP * c), GROUP * (c + 1))):
            outgoing[i].wait_recv()
            forwards[i] = forward(i)


    padded = jnp.concatenate(
        [routes_t.astype(F32), gates_t_ref[...]], axis=0)
    padded = jnp.transpose(jnp.concatenate([padded, jnp.zeros((8, 64), F32)], axis=1))[:TOK, :]
    routes = padded[:, :TOPK].astype(jnp.int32)
    gates = padded[:, TOPK:]
    expert_of = offset_expert(iota((TOK, CHIPS), 1), x_hi, z)
    hits = jnp.zeros((TOK, CHIPS), F32)
    for k in range(TOPK):
        hits = hits + (routes[:, k : k + 1] == expert_of).astype(F32)
    earlier = (iota((TOK, TOK), 1) < iota((TOK, TOK), 0)).astype(BF16)
    slots = jnp.where(hits > 0.5, dot(earlier, hits.astype(BF16)), 100.0)
    spread = (iota((CHIPS, 256), 0) == (iota((CHIPS, 256), 1) >> 4)).astype(BF16)
    slots = dot(slots.astype(BF16), spread).astype(jnp.int32)
    column_expert = offset_expert(iota((TOK, 256), 1) >> 4, x_hi, z)
    weight = jnp.zeros((TOK, 256), F32)
    for k in range(TOPK):
        weight = weight + jnp.where(routes[:, k : k + 1] == column_expert, gates[:, k : k + 1], 0.0)
    place = iota((TOK, 256), 1) & 15
    combine_main = jnp.concatenate(split3(jnp.where(slots == place, weight, 0.0)), axis=0)
    combine_tail = [
        jnp.concatenate(split3(jnp.where((slots - 16 == (place & 3)) & ((place >> 2) == j), weight, 0.0)), axis=0)
        for j in range(4)
    ]

    wide = iota((512, 512), 0)
    perm[:512, :] = (iota((512, 512), 1) == 4 * (wide & 127) + (wide >> 7)).astype(F32).astype(BF16)
    narrow = iota((256, 512), 0)
    perm[512:768, :] = (iota((256, 512), 1) == 4 * (narrow & 63) + (narrow >> 6)).astype(F32).astype(BF16)
    wg[D:, :] = jnp.zeros((DP - D, FF), BF16)
    wu[D:, :] = jnp.zeros((DP - D, FF), BF16)
    wd[:, D:] = jnp.zeros((FF, DP - D), BF16)
    loads[3].wait()
    turn(gct, gc, D, 192)
    code_planes(gc, planes, D, 192)
    weight_rows(planes, gs, perm, wg, D, 192, 288)
    loads[4].wait()
    turn(uct, uc, D, 192)
    code_planes(uc, planes, D, 192)
    weight_rows(planes, us, perm, wu, D, 192, 288)
    loads[5].wait()
    turn(dct, dc, FF, 360)
    code_planes(dc, planes, FF, 360)
    arrive(CHIPS // GROUP - 1)
    weight_rows(planes, ds, perm, wd, FF, 360, 256)

    side = 32 * GROUP
    a, b = iota((side, side), 0), iota((side, side), 1)
    moved_to = lambda r: ((r >> 2) % (2 * GROUP)) * 16 + (r // (8 * GROUP)) * 4 + (r & 3)
    to_rows = (b == moved_to(a)).astype(F32).astype(BF16)
    to_block = (a == moved_to(b)).astype(F32).astype(BF16)

    sent_pieces = {}
    sent_results = []

    def finish(c):
        sent_pieces[c].wait_recv()
        for i in range(GROUP * c, GROUP * (c + 1)):
            total = (p_mine[i].astype(F32) + p_in[i].astype(F32)).astype(BF16)
            if i == 0:
                ret[0] = total
            else:
                result[i] = total
        for i in reversed(range(max(1, GROUP * c), GROUP * (c + 1))):
            copy = pltpu.make_async_remote_copy(
                src_ref=result.at[i], dst_ref=ret.at[i], send_sem=res_sem.at[i], recv_sem=ret_sem.at[i],
                device_id=source(i), device_id_type=MESH)
            copy.start()
            sent_results.append(copy)

    for c in reversed(range(CHIPS // GROUP)):
        if c < CHIPS // GROUP - 1:
            arrive(c)
        for i in range(GROUP * c, GROUP * (c + 1)):
            forwards[i].wait_recv()
        if c == 0:
            mine[0] = send[0]

        def both(lo, hi):
            return jnp.concatenate(
                [ref[GROUP * c : GROUP * (c + 1), lo:hi, :].reshape(16 * GROUP, 128) for ref in (mine, other)],
                axis=0)

        main = jnp.concatenate([both(16 * j, 16 * j + 16) for j in range(12)], axis=1)
        tails = []
        for g in range(3):
            moved = dot(to_rows, both(192 + 16 * g, 208 + 16 * g)).astype(BF16)
            tails += [moved[8 * GROUP * j : 8 * GROUP * (j + 1), :] for j in range(4)]
        x = jnp.concatenate([main, jnp.concatenate(tails, axis=1)], axis=0)
        gate_act = dot(x, wg[...])
        up_act = dot(x, wu[...])
        active = ((up_act + 1.0) * gate_act * jax.nn.sigmoid(1.702 * gate_act)).astype(BF16)
        y = dot(active, wd[...]).astype(BF16)
        for j in range(12):
            tile = y[:side, 128 * j : 128 * j + 128]
            p_mine[GROUP * c : GROUP * (c + 1), 16 * j : 16 * j + 16, :] = tile[: side // 2].reshape(GROUP, 16, 128)
            p_other[GROUP * c : GROUP * (c + 1), 16 * j : 16 * j + 16, :] = tile[side // 2 :].reshape(GROUP, 16, 128)
        for g in range(3):
            tiles = jnp.concatenate([y[side:, 128 * (4 * g + j) : 128 * (4 * g + j + 1)] for j in range(4)], axis=0)
            back = dot(to_block, tiles).astype(BF16)
            p_mine[GROUP * c : GROUP * (c + 1), 192 + 16 * g : 208 + 16 * g, :] = back[: side // 2].reshape(GROUP, 16, 128)
            p_other[GROUP * c : GROUP * (c + 1), 192 + 16 * g : 208 + 16 * g, :] = back[side // 2 :].reshape(GROUP, 16, 128)
        copy = pltpu.make_async_remote_copy(
            src_ref=p_other.at[pl.ds(GROUP * c, GROUP)], dst_ref=p_in.at[pl.ds(GROUP * c, GROUP)],
            send_sem=pout_sem.at[c], recv_sem=pin_sem.at[c], device_id=partner, device_id_type=MESH)
        copy.start()
        sent_pieces[c] = copy
        finish(c)

    for copy in sent_results:
        copy.wait_recv()
    for j in range(12):
        part = dot(combine_main, ret[:, 16 * j : 16 * j + 16, :].reshape(256, 128))
        g = j // 4
        part = part + dot(combine_tail[j % 4], ret[:, 192 + 16 * g : 208 + 16 * g, :].reshape(256, 128))
        mixed = part[:TOK] + part[TOK : 2 * TOK] + part[2 * TOK :]
        lo, hi = 128 * j, min(128 * j + 128, D)
        out_ref[:, lo:hi] = branch_ref[:, lo:hi] + mixed[:, : hi - lo]

    for copy in list(outgoing.values()) + list(forwards.values()) + list(sent_pieces.values()) + sent_results + kv_gather.copies + ow_gather.copies + ow_gather.given:
        copy.wait_send()


def local(
    queries, keys, values, sinks, out_weight, norm_gain, routes, gates,
    gate_codes, up_codes, down_codes, gate_scales, up_scales, down_scales,
):
    vmem = pl.BlockSpec(memory_space=pltpu.VMEM)
    hbm = pl.BlockSpec(memory_space=pl.ANY)
    dma = pltpu.SemaphoreType.DMA
    blocks = pltpu.VMEM((CHIPS, BLK, 128), BF16)
    out = pl.pallas_call(
        layer_kernel,
        out_shape=jax.ShapeDtypeStruct((TOK, D), F32),
        in_specs=[hbm] * 3 + [pl.BlockSpec(memory_space=pltpu.SMEM), hbm] + [vmem] * 3 + [hbm] * 3 + [vmem] * 3,
        out_specs=vmem,
        scratch_shapes=[
            pltpu.VMEM((TOK, QH * HD), BF16),
            pltpu.VMEM((16, TOK, 512), BF16),
            pltpu.VMEM((QH * TOK, 256), BF16),
            pltpu.VMEM((QH * TOK, 128), F32),
            pltpu.VMEM((QH * TOK, 128), F32),
            pltpu.VMEM((QH * TOK, 256), F32),
            pltpu.VMEM((QH // 2, TOK, 128), BF16),
            pltpu.VMEM((64, 32, D), BF16),
            pltpu.VMEM((TOK, D), F32),
            pltpu.VMEM((TOK, DP), BF16),
            pltpu.VMEM((192, D), jnp.int32),
            pltpu.VMEM((192, D), jnp.int32),
            pltpu.VMEM((360, FF), jnp.int32),
            pltpu.VMEM((D, 192), jnp.int32),
            pltpu.VMEM((D, 192), jnp.int32),
            pltpu.VMEM((FF, 360), jnp.int32),
            pltpu.VMEM((D, DP), BF16),
            pltpu.VMEM((FF, 512), BF16),
            pltpu.VMEM((DP, FF), BF16),
            pltpu.VMEM((DP, FF), BF16),
            pltpu.VMEM((FF, DP), BF16),
            blocks, blocks, blocks, blocks, blocks, blocks, blocks, blocks,
            dma((7,)), dma((15,)), dma((15,)), dma((30,)), dma((30,)), dma((32,)), dma((32,)),
            dma((CHIPS,)), dma((CHIPS,)), dma((CHIPS,)), dma((CHIPS,)), dma((CHIPS // GROUP,)), dma((CHIPS // GROUP,)),
            dma((CHIPS,)), dma((CHIPS,)),
        ],
        compiler_params=pltpu.CompilerParams(collective_id=0, has_side_effects=True, vmem_limit_bytes=60 * 1024 * 1024),
        name="layer",
    )(
        queries[0], keys[0], values[0], sinks, out_weight.reshape(2, 32, D), norm_gain, routes[0].T, gates[0].T,
        gate_codes[0].T, up_codes[0].T, down_codes[0].T, jnp.swapaxes(gate_scales, 0, 1), jnp.swapaxes(up_scales, 0, 1), down_scales[0],
    )
    return out.astype(BF16)[None]


def solution(mesh):
    return jax.shard_map(
        local,
        mesh=mesh,
        in_specs=(
            P("exp", "ctx", None),
            P("exp", "ctx", None),
            P("exp", "ctx", None),
            P(),
            P("exp", None),
            P(),
            P("exp", "ctx", None),
            P("exp", "ctx", None),
            P("exp", None, None),
            P("exp", None, None),
            P("exp", None, None),
            P("exp", None, None),
            P("exp", None, None),
            P("exp", None, None),
        ),
        out_specs=P("exp", "ctx", None),
        check_vma=False,
    )
```
